128 devices in a mesh: segment: 2 (over z_lo), expert: 32 (over x, y, core), dp: 2 (over z_hi).
Axes of the slice: x: 4, y: 4, z: 4 (z_hi: 2, z_lo: 2; z = z_hi * 2 + z_lo), core: 2. Of those that a mesh axis runs over, the one named last changes fastest.
Arguments:
- features: bfloat16 [2, 4096, 512], P(None, ('expert', 'dp')), may hold values from -6 to 6
- routes: int32 [2, 4096, 2], P(None, ('expert', 'dp')), may hold values from 0 to 31, all different within a row; in each aligned block of 64 rows (0 to 63, 64 to 127, ..., all dimensions but the last counted through in order) at most 8 rows name the same one
- arm_ids: int32 [2, 4096], P(None, ('expert', 'dp')), may hold values from 0 to 5
- targets: float32 [2, 4096], P(None, ('expert', 'dp')), may hold values from -6 to 6
- trunk_gain: float32 [512], replicated, may hold values from 0.5 to 1.5
- gate_weight: bfloat16 [32, 512, 4096], P('expert', None, ('segment', 'dp')), may hold values from -0.25 to 0.25
- up_weight: bfloat16 [32, 512, 4096], P('expert', None, ('segment', 'dp')), may hold values from -0.25 to 0.25
- down_weight: bfloat16 [32, 4096, 512], P('expert', ('segment', 'dp')), may hold values from -0.09375 to 0.09375
- tower_in: bfloat16 [7, 512, 8192], P(None, None, ('segment', 'expert', 'dp')), may hold values from -0.25 to 0.25
- tower_out: bfloat16 [7, 8192], P(None, ('segment', 'expert', 'dp')), may hold values from -0.0625 to 0.0625
Outputs:
- grad_gate: bfloat16 [32, 512, 4096], P('expert', None, ('segment', 'dp'))
- grad_up: bfloat16 [32, 512, 4096], P('expert', None, ('segment', 'dp'))
- grad_down: bfloat16 [32, 4096, 512], P('expert', ('segment', 'dp'))
- grad_tower_in: bfloat16 [7, 512, 8192], P(None, None, ('segment', 'expert', 'dp'))
- grad_tower_out: bfloat16 [7, 8192], P(None, ('segment', 'expert', 'dp'))
- grad_gain: float32 [512], replicated
The draws below stay inside these ranges and needn't reach their ends.
Inputs may be any that keep to these rules, and one draw needn't show every extreme that they name: `routes`: each row names 2 different experts; within every micro-batch, each aligned block of 64 rows names any one expert at most 8 times, a bound that some block reaches.
All inputs are finite; a program needn't handle non-finite values.
Results may differ from the reference program's by a relative error of at most 0.023.
Values may be sent and summed in bfloat16 or wider, within the bound.
A program may use at most 256 MiB of HBM per device.

```python
import math
import jax
import jax.numpy as jnp
import numpy as np
from jax import lax

D = 512
FFE = 4096
TW = 8192
TOP = 2
OUTCOMES = 6
MB = 2
ROWS_DEV = 64
EXPERTS = 32
TOWERS = 7
ROWS = 4096
CAP = 8
N_EXPERT = 32
N_DP = 2


def place_ends(array, stream_key, smallest, top_value):
    index_at = [jax.random.randint(jax.random.fold_in(stream_key, axis), (), 0, length) for axis, length in enumerate(array.shape)]
    longest = array.shape.index(max(array.shape))
    next_to = index_at[:longest] + [(index_at[longest] + 1) % array.shape[longest]] + index_at[longest + 1:]
    return array.at[tuple(index_at)].set(smallest).at[tuple(next_to)].set(top_value)


def level_of(rng, shape, split, least, high):
    loudness, own = 1.0, jax.random.fold_in(rng, 6)
    for axis_at, parts in split:
        heights = jnp.exp(jax.random.uniform(jax.random.fold_in(own, axis_at), (parts,), jnp.float32, least / len(split), high / len(split)))
        loudness = loudness * jnp.repeat(heights, shape[axis_at] // parts).reshape([-1 if axis == axis_at else 1 for axis in range(len(shape))])
    return loudness


def deal_out(stream_key, own, number, rows, amount, top, reach, skew):
    sequence = jax.random.permutation(stream_key, amount)
    packed, ordinary = portions_of(amount, rows * top, reach, skew, True), portions_of(amount, rows * top, reach, skew, False)
    places = jnp.arange(amount)

    def named(sizes, offset_by):
        used = int((sizes > 0).sum())
        fixed = max(1, used // 4)
        moved = fixed + (places - fixed + offset_by * (used - fixed)) % max(1, amount - fixed)
        return jnp.zeros((amount,), jnp.int32).at[sequence[jnp.where(places < fixed, places, moved)]].set(jnp.asarray(sizes, jnp.int32))

    sizes = jnp.where(number % 4 == 0, named(packed, number // 4), named(ordinary, number - number // 4 - 1))
    mixed = jax.random.permutation(jax.random.fold_in(own, 3), amount)
    source_of, sink = mixed[0:amount // 2 * 2:2], mixed[1:amount // 2 * 2:2]
    room = jnp.minimum(sizes[source_of] - 1, reach - sizes[sink]) // 2
    room = jnp.where((source_of == sequence[0]) | (sink == sequence[0]) | (sizes[sink] == 0), 0, jnp.maximum(room, 0))
    moved = jax.random.randint(jax.random.fold_in(own, 4), (amount // 2,), 0, 1 << 20) % (room + 1)
    sizes = sizes.at[source_of].add(-moved).at[sink].add(moved)
    labels = jnp.searchsorted(jnp.cumsum(sizes), jnp.arange(rows * top), side="right").astype(jnp.int32)
    listing = labels.reshape(top, rows).T
    listing = listing[jax.random.permutation(jax.random.fold_in(own, 1), rows)]
    offset_by = jax.random.randint(jax.random.fold_in(own, 2), (rows, 1), 0, top)
    return jnp.take_along_axis(listing, (jnp.arange(top)[None, :] + offset_by) % top, axis=1)


def portions_of(amount, total, most, lean, full):
    portions = [(1 << 20) // math.isqrt(rank ** lean) + 1 for rank in range(1, amount + 1)]
    largest = most if full else min(most, max(-(-total // amount), total * portions[0] // sum(portions)))
    least = 1 if total - largest >= amount - 1 else 0
    given, spare = [largest] + [least] * (amount - 1), total - largest - least * (amount - 1)
    while spare > 0:
        candidates = [i for i in range(1, amount) if given[i] < largest] or [i for i in range(1, amount) if given[i] < most]
        pool, remaining = sum([portions[i] for i in candidates]), spare
        for i in candidates:
            more = min(most - given[i], max(1, remaining * portions[i] // pool), spare)
            given[i] = given[i] + more
            spare = spare - more
    return np.array(given)


def gaussian(stream_key, dims, width, limit, split=(), kind=jnp.bfloat16):
    drawn = width * jax.random.normal(stream_key, dims, jnp.float32)
    if split:
        drawn = drawn * level_of(stream_key, dims, split, -0.22, 0.18)
    return jnp.clip(drawn, -limit, limit).astype(kind)


def setup_inputs(seed: int = 0) -> dict:
    streams_of = jax.random.split(jax.random.key(seed), 11)
    features = gaussian(streams_of[0], (MB, ROWS, D), 1.0, 6.0, ((1, 64),))
    routes_keys = jax.random.split(jax.random.fold_in(streams_of[1], 1), MB * ROWS // ROWS_DEV)
    routes_turns = jax.random.permutation(jax.random.fold_in(streams_of[1], 3), MB * ROWS // ROWS_DEV)
    routes = jax.vmap(lambda own, number: deal_out(jax.random.fold_in(streams_of[1], 2), own, number, ROWS_DEV, EXPERTS, TOP, CAP, 1))(routes_keys, routes_turns).reshape((MB, ROWS, TOP))
    arm_ids = place_ends(jax.random.randint(streams_of[2], (MB, ROWS), 0, OUTCOMES), jax.random.fold_in(streams_of[2], 1), 0, OUTCOMES - 1).astype(jnp.int32)
    targets = gaussian(streams_of[3], (MB, ROWS), 1.0, 6.0, ((1, 64),), jnp.float32)
    trunk_gain = jnp.clip(1.0 + 0.1 * jax.random.normal(streams_of[4], (D,), jnp.float32), 0.5, 1.5)
    gate_weight = gaussian(streams_of[5], (EXPERTS, D, FFE), D ** -0.5, 0.25, ((0, 32), (2, 4)))
    up_weight = gaussian(streams_of[6], (EXPERTS, D, FFE), D ** -0.5, 0.25, ((0, 32), (2, 4)))
    down_weight = gaussian(streams_of[7], (EXPERTS, FFE, D), FFE ** -0.5, 0.09375, ((0, 32), (1, 4)))
    tower_in = gaussian(streams_of[8], (TOWERS, D, TW), D ** -0.5, 0.25, ((2, 128),))
    tower_out = gaussian(streams_of[9], (TOWERS, TW), TW ** -0.5, 0.0625, ((1, 128),))
    return {"features": features, "routes": routes, "arm_ids": arm_ids, "targets": targets, "trunk_gain": trunk_gain, "gate_weight": gate_weight, "up_weight": up_weight, "down_weight": down_weight, "tower_in": tower_in, "tower_out": tower_out}


EPSILON = 1e-06

def silu_slope(value):
    sig_value = jax.nn.sigmoid(value)
    return sig_value * (1.0 + value * (1.0 - sig_value))

def widen_value(value):
    return lax.optimization_barrier(value).astype(jnp.float32)

def replica_sum(partials):
    return lax.optimization_barrier(jnp.sum(widen_value(partials.astype(jnp.bfloat16)), axis=0)).astype(jnp.bfloat16)

def expert_forward(inputs, w_gate, w_up):
    gate_pre = jnp.dot(inputs, w_gate, preferred_element_type=jnp.float32)
    up_pre = jnp.dot(inputs, w_up, preferred_element_type=jnp.float32)
    return (gate_pre, up_pre, (jax.nn.silu(gate_pre) * up_pre).astype(jnp.bfloat16))

def reference(features, routes, arm_ids, targets, trunk_gain, gate_weight, up_weight, down_weight, tower_in, tower_out):
    batches, rows_all, feature_width = features.shape
    blocks = N_EXPERT * N_DP
    loss_scale = (batches * rows_all) ** (-0.5)
    wide_rows = features.astype(jnp.float32)
    scaled = wide_rows * lax.rsqrt(lax.optimization_barrier(jnp.mean(wide_rows * wide_rows, axis=-1, keepdims=True)) + EPSILON)
    normed = (scaled * trunk_gain).astype(jnp.bfloat16)
    chosen = routes.reshape(batches, blocks, ROWS_DEV * TOP)
    onehot = (chosen[..., None] == jnp.arange(EXPERTS, dtype=jnp.int32)).astype(jnp.int32)
    before = jnp.cumsum(onehot, axis=2) - onehot
    slot_rank = lax.optimization_barrier(jnp.sum(before * onehot, axis=3)).astype(jnp.int32)
    batch_ids = jnp.broadcast_to(jnp.arange(batches, dtype=jnp.int32)[:, None, None], chosen.shape)
    block_ids = jnp.broadcast_to(jnp.arange(blocks, dtype=jnp.int32)[None, :, None], chosen.shape)
    places = (chosen, batch_ids, block_ids, slot_rank)
    empty_slots = jnp.zeros((EXPERTS, batches, blocks, CAP, feature_width), jnp.bfloat16)
    spread = jnp.repeat(normed.reshape(batches, blocks, ROWS_DEV, feature_width), TOP, axis=2)
    buffer = empty_slots.at[places].set(spread)

    def run_expert(operands):
        inputs, w_gate, w_up, w_down = operands
        flat_in = inputs.reshape(-1, feature_width)
        _, _, active = expert_forward(flat_in, w_gate, w_up)
        produced = jnp.dot(active, w_down, preferred_element_type=jnp.float32).astype(jnp.bfloat16)
        return produced.reshape(inputs.shape)
    produced = lax.map(run_expert, (buffer, gate_weight, up_weight, down_weight))
    picked = widen_value(produced[places]).reshape(batches, blocks, ROWS_DEV, TOP, feature_width)
    mixed = (wide_rows.reshape(batches, blocks, ROWS_DEV, feature_width) + lax.optimization_barrier(jnp.sum(picked, axis=3))).astype(jnp.bfloat16)
    flat_mixed = mixed.reshape(-1, feature_width)
    grouped_mixed = widen_value(mixed).reshape(batches, N_EXPERT, N_DP, ROWS_DEV, feature_width)
    flat_arms = arm_ids.reshape(-1)
    flat_targets = targets.reshape(-1).astype(jnp.float32)
    treated = (flat_arms != 0).astype(jnp.float32)

    def run_tower(grad_carry, operands):
        w_in, w_out, tower_index = operands
        pre_act = jnp.dot(flat_mixed, w_in, preferred_element_type=jnp.float32)
        hidden = jax.nn.silu(pre_act).astype(jnp.bfloat16)
        tower_value = jnp.dot(hidden, w_out, preferred_element_type=jnp.float32)
        propensity = loss_scale * (jax.nn.sigmoid(tower_value) - treated)
        outcome = loss_scale * (tower_value - flat_targets) * (flat_arms == tower_index - 1).astype(jnp.float32)
        grad_value = jnp.where(tower_index == 0, propensity, outcome)
        grad_pre = (grad_value[:, None] * w_out.astype(jnp.float32)[None, :] * silu_slope(pre_act)).astype(jnp.bfloat16)
        grad_carry = grad_carry + jnp.dot(grad_pre, w_in.T, preferred_element_type=jnp.float32)
        shaped_pre = widen_value(grad_pre).reshape(batches, N_EXPERT, N_DP, ROWS_DEV, -1)
        part_in = jnp.einsum('bedrk,bedrj->dkj', grouped_mixed, shaped_pre)
        shaped_hidden = widen_value(hidden).reshape(batches, N_EXPERT, N_DP, ROWS_DEV, -1)
        shaped_grad = widen_value(grad_value.astype(jnp.bfloat16)).reshape(batches, N_EXPERT, N_DP, ROWS_DEV)
        part_out = jnp.einsum('bedr,bedrj->dj', shaped_grad, shaped_hidden)
        return (grad_carry, (replica_sum(part_in), replica_sum(part_out)))
    start_carry = jnp.zeros((batches * rows_all, feature_width), jnp.float32)
    tower_ids = jnp.arange(TOWERS, dtype=jnp.int32)
    grad_carry, tower_grads = lax.scan(run_tower, start_carry, (tower_in, tower_out, tower_ids))
    grad_tower_in, grad_tower_out = tower_grads
    grad_mixed = grad_carry.astype(jnp.bfloat16)
    grad_spread = jnp.repeat(grad_mixed.reshape(batches, blocks, ROWS_DEV, feature_width), TOP, axis=2)
    grad_buffer = empty_slots.at[places].set(grad_spread)

    def back_expert(operands):
        inputs, grads, w_gate, w_up, w_down = operands
        flat_in = inputs.reshape(-1, feature_width)
        flat_grad = grads.reshape(-1, feature_width)
        gate_pre, up_pre, active = expert_forward(flat_in, w_gate, w_up)
        grad_active = jnp.dot(flat_grad, w_down.T, preferred_element_type=jnp.float32)
        grad_gate_pre = (grad_active * up_pre * silu_slope(gate_pre)).astype(jnp.bfloat16)
        grad_up_pre = (grad_active * jax.nn.silu(gate_pre)).astype(jnp.bfloat16)
        grad_part = jnp.dot(grad_gate_pre, w_gate.T, preferred_element_type=jnp.float32)
        grad_part = (grad_part + jnp.dot(grad_up_pre, w_up.T, preferred_element_type=jnp.float32)).astype(jnp.bfloat16)

        def per_replica(left_side, right_side):
            left_wide = widen_value(left_side).reshape(batches, N_EXPERT, N_DP, CAP, -1)
            right_wide = widen_value(right_side).reshape(batches, N_EXPERT, N_DP, CAP, -1)
            return replica_sum(jnp.einsum('bedck,bedcf->dkf', left_wide, right_wide))
        return (per_replica(flat_in, grad_gate_pre), per_replica(flat_in, grad_up_pre), per_replica(active, flat_grad), grad_part.reshape(inputs.shape))
    grad_gate, grad_up, grad_down, grad_slots = lax.map(back_expert, (buffer, grad_buffer, gate_weight, up_weight, down_weight))
    grad_rows = lax.optimization_barrier(jnp.sum(widen_value(grad_slots[places]).reshape(batches, blocks, ROWS_DEV, TOP, feature_width), axis=3))
    grad_gain = lax.optimization_barrier(jnp.sum(grad_rows * scaled.reshape(batches, blocks, ROWS_DEV, feature_width), axis=(0, 1, 2)))
    return (grad_gate, grad_up, grad_down, grad_tower_in, grad_tower_out, grad_gain)
```

```python
import functools

import jax
import jax.numpy as jnp
from jax import lax
from jax.experimental import pallas as pl
from jax.experimental.pallas import tpu as pltpu
from jax.sharding import PartitionSpec as P

EPSILON = 1e-06
MESH = pl.DeviceIdType.MESH
VMEM = pltpu.VMEM
F32 = jnp.float32
BF16 = jnp.bfloat16


def place():
    return lax.axis_index("segment"), lax.axis_index("expert"), lax.axis_index("dp")


def remote(src, dst, send, recv, seg, expert, dp):
    return pltpu.make_async_remote_copy(
        src_ref=src,
        dst_ref=dst,
        send_sem=send,
        recv_sem=recv,
        device_id=(seg, expert, dp),
        device_id_type=MESH,
    )


def meet_plane(seg, me, dp, count):
    barrier = pltpu.get_barrier_semaphore()

    def greet(i, carry):
        pl.semaphore_signal(
            barrier, inc=1, device_id=(seg, lax.rem(me + i, count), dp), device_id_type=MESH
        )
        return carry

    lax.fori_loop(1, count, greet, 0)
    return barrier


def meet_all(seg, me, dp, count):
    barrier = pltpu.get_barrier_semaphore()
    all_count = 4 * count

    def greet(i, carry):
        e, z = i // 4, lax.rem(i, 4)
        pl.semaphore_signal(
            barrier,
            inc=1,
            device_id=(
                lax.rem(seg + lax.rem(z, 2), 2),
                lax.rem(me + e, count),
                lax.rem(dp + z // 2, 2),
            ),
            device_id_type=MESH,
        )
        return carry

    lax.fori_loop(1, all_count, greet, 0)
    pl.semaphore_wait(barrier, all_count - 1)


def wait_bytes(ref, sem):
    pltpu.make_async_copy(ref, ref, sem).wait()


def call(kernel, out_shape, scratch, ident, *args):
    return pl.pallas_call(
        kernel,
        out_shape=out_shape,
        in_specs=[pl.BlockSpec(memory_space=VMEM)] * len(args),
        out_specs=jax.tree.map(lambda _: pl.BlockSpec(memory_space=VMEM), out_shape),
        scratch_shapes=scratch,
        compiler_params=pltpu.CompilerParams(collective_id=ident, has_side_effects=True),
    )(*args)


def dispatch_kernel(count, slots, aux, got, got_aux, send, recv, aux_send, aux_recv):
    seg, me, dp = place()
    barrier = meet_plane(seg, me, dp, count)

    def greet(i, carry):
        pl.semaphore_signal(barrier, inc=1, device_id=(1 - seg, i, 1 - dp), device_id_type=MESH)
        return carry

    lax.fori_loop(0, count, greet, 0)
    pl.semaphore_wait(barrier, 2 * count - 1)
    mine = dp * count + me

    def start(i, carry):
        to = lax.rem(me + i, count)
        remote(slots.at[to], got.at[mine], send, recv, 1 - seg, to, 1 - dp).start()

        @pl.when(i > 0)
        def _():
            remote(slots.at[to], got.at[mine], send, recv, seg, to, dp).start()
            remote(aux, got_aux.at[me], aux_send, aux_recv, seg, to, dp).start()

        return carry

    lax.fori_loop(0, count, start, 0)
    pltpu.make_async_copy(slots.at[me], got.at[mine], recv).start()
    pltpu.make_async_copy(aux, got_aux.at[me], aux_recv).start()
    wait_bytes(got_aux, aux_recv)
    wait_bytes(got_aux.at[pl.ds(0, count - 1)], aux_send)
    wait_bytes(got, recv)
    wait_bytes(got.at[pl.ds(0, 2 * count - 1)], send)


def dispatch(slots, aux):
    count = slots.shape[0]
    return call(
        functools.partial(dispatch_kernel, count),
        (
            jax.ShapeDtypeStruct((2 * count,) + slots.shape[1:], slots.dtype),
            jax.ShapeDtypeStruct((count,) + aux.shape, aux.dtype),
        ),
        [pltpu.SemaphoreType.DMA(())] * 4,
        0,
        slots,
        aux,
    )


def giveback_kernel(count, sent, got, send, recv):
    seg, me, dp = place()
    meet_all(seg, me, dp, count)
    mine = (dp * 2 + seg) * count + me

    def start(i, carry):
        e, z = lax.rem(me + i // 4, count), lax.rem(i, 4)
        to_seg, to_dp = lax.rem(seg + lax.rem(z, 2), 2), lax.rem(dp + z // 2, 2)
        block = (to_dp * count + e) * 2 + to_seg
        remote(sent.at[block], got.at[mine], send, recv, to_seg, e, to_dp).start()
        return carry

    lax.fori_loop(1, 4 * count, start, 0)
    pltpu.make_async_copy(sent.at[(dp * count + me) * 2 + seg], got.at[mine], recv).start()
    wait_bytes(got, recv)
    wait_bytes(got.at[pl.ds(0, 4 * count - 1)], send)


def giveback(sent, count):
    return call(
        functools.partial(giveback_kernel, count),
        jax.ShapeDtypeStruct(sent.shape, sent.dtype),
        [pltpu.SemaphoreType.DMA(())] * 2,
        1,
        sent,
    )


def gather_kernel(count, rows, got, first_send, first_recv, pass_send, pass_recv):
    seg, me, dp = place()
    barrier = meet_plane(seg, me, dp, count)
    pl.semaphore_wait(barrier, count - 1)
    chips = count // 2
    chip, core = me // 2, lax.rem(me, 2)
    mine = core * chips + chip

    def start(i, carry):
        to = lax.rem(chip + i, chips)
        remote(rows, got.at[mine], first_send, first_recv.at[i], seg, to * 2 + core, dp).start()
        return carry

    lax.fori_loop(1, chips, start, 0)
    own = pltpu.make_async_copy(rows, got.at[mine], first_recv.at[0])
    own.start()
    remote(rows, got.at[mine], pass_send, pass_recv, seg, chip * 2 + 1 - core, dp).start()
    own.wait()

    def relay(i, carry):
        source = core * chips + lax.rem(chip - i + chips, chips)
        block = got.at[source]
        wait_bytes(block, first_recv.at[i])
        remote(block, block, pass_send, pass_recv, seg, chip * 2 + 1 - core, dp).start()
        return carry

    lax.fori_loop(1, chips, relay, 0)
    wait_bytes(got.at[pl.ds((1 - core) * chips, chips)], pass_recv)
    wait_bytes(got.at[pl.ds(0, chips)], pass_send)
    wait_bytes(got.at[pl.ds(0, chips - 1)], first_send)


def gather(rows, count):
    return call(
        functools.partial(gather_kernel, count),
        jax.ShapeDtypeStruct((count,) + rows.shape, rows.dtype),
        [
            pltpu.SemaphoreType.DMA(()),
            pltpu.SemaphoreType.DMA((count // 2,)),
            pltpu.SemaphoreType.DMA(()),
            pltpu.SemaphoreType.DMA(()),
        ],
        2,
        rows,
    )


def share_kernel(count, value, got, send, recv):
    seg, me, dp = place()
    barrier = meet_plane(seg, me, dp, count)
    pl.semaphore_wait(barrier, count - 1)

    def start(i, carry):
        to = lax.rem(me + i, count)
        remote(value, got.at[me], send, recv, seg, to, dp).start()
        return carry

    lax.fori_loop(1, count, start, 0)
    pltpu.make_async_copy(value, got.at[me], recv).start()
    wait_bytes(got, recv)
    wait_bytes(got.at[pl.ds(0, count - 1)], send)


def share(value, count):
    return call(
        functools.partial(share_kernel, count),
        jax.ShapeDtypeStruct((count,) + value.shape, value.dtype),
        [pltpu.SemaphoreType.DMA(())] * 2,
        3,
        value,
    )


def scatter_kernel(count, parts, out, pair, paired, got, pair_send, pair_recv, send, recv):
    seg, me, dp = place()
    barrier = meet_plane(seg, me, dp, count)
    pl.semaphore_wait(barrier, count - 1)
    chips = count // 2
    chip, core = me // 2, lax.rem(me, 2)

    def swap(i, carry):
        to = lax.rem(chip + chips - i, chips)
        remote(
            parts.at[(1 - core) * chips + to],
            pair.at[to],
            pair_send,
            pair_recv.at[to],
            seg,
            chip * 2 + 1 - core,
            dp,
        ).start()
        return carry

    lax.fori_loop(1, chips + 1, swap, 0)

    def forward(i, carry):
        to = lax.rem(chip + chips - i, chips)
        wait_bytes(pair.at[to], pair_recv.at[to])
        paired[to] = (
            parts[core * chips + to].astype(F32) + pair[to].astype(F32)
        ).astype(BF16)
        remote(paired.at[to], got.at[chip], send, recv, seg, to * 2 + core, dp).start()
        return carry

    lax.fori_loop(1, chips, forward, 0)
    wait_bytes(pair.at[chip], pair_recv.at[chip])
    got[chip] = (parts[core * chips + chip].astype(F32) + pair[chip].astype(F32)).astype(BF16)
    wait_bytes(got.at[pl.ds(0, chips - 1)], recv)
    total = got[0].astype(F32)
    for i in range(1, chips):
        total = total + got[i].astype(F32)
    out[...] = total.astype(BF16)
    wait_bytes(pair, pair_send)
    wait_bytes(got.at[pl.ds(0, chips - 1)], send)


def scatter(parts):
    count = parts.shape[0]
    half = (count // 2,) + parts.shape[1:]
    return call(
        functools.partial(scatter_kernel, count),
        jax.ShapeDtypeStruct(parts.shape[1:], parts.dtype),
        [
            pltpu.VMEM(half, BF16),
            pltpu.VMEM(half, BF16),
            pltpu.VMEM(half, BF16),
            pltpu.SemaphoreType.DMA(()),
            pltpu.SemaphoreType.DMA((count // 2,)),
            pltpu.SemaphoreType.DMA(()),
            pltpu.SemaphoreType.DMA(()),
        ],
        4,
        parts,
    )


def spread_kernel(count, slots, got, send, recv):
    seg, me, dp = place()
    meet_all(seg, me, dp, count)
    mine = (dp * count + me) * 2 + seg

    def start(i, carry):
        e, z = lax.rem(me + i // 4, count), lax.rem(i, 4)
        to_seg, to_dp = lax.rem(seg + lax.rem(z, 2), 2), lax.rem(dp + z // 2, 2)
        remote(slots.at[e], got.at[mine], send, recv, to_seg, e, to_dp).start()
        return carry

    lax.fori_loop(1, 4 * count, start, 0)
    pltpu.make_async_copy(slots.at[me], got.at[mine], recv).start()
    wait_bytes(got, recv)
    wait_bytes(got.at[pl.ds(0, 4 * count - 1)], send)


def spread(slots):
    count = slots.shape[0]
    return call(
        functools.partial(spread_kernel, count),
        jax.ShapeDtypeStruct((4 * count,) + slots.shape[1:], slots.dtype),
        [pltpu.SemaphoreType.DMA(())] * 2,
        5,
        slots,
    )


def add_all_kernel(count, part, out, got, send, recv):
    seg, me, dp = place()
    meet_all(seg, me, dp, count)
    mine = (dp * count + me) * 2 + seg

    def start(i, carry):
        e, z = lax.rem(me + i // 4, count), lax.rem(i, 4)
        to_seg, to_dp = lax.rem(seg + lax.rem(z, 2), 2), lax.rem(dp + z // 2, 2)
        remote(part, got.at[mine], send, recv, to_seg, e, to_dp).start()
        return carry

    lax.fori_loop(1, 4 * count, start, 0)
    pltpu.make_async_copy(part, got.at[mine], recv).start()
    wait_bytes(got, recv)
    out[...] = jnp.sum(got[...], axis=0)
    wait_bytes(got.at[pl.ds(0, 4 * count - 1)], send)


def add_all(part, count):
    return call(
        functools.partial(add_all_kernel, count),
        jax.ShapeDtypeStruct(part.shape, part.dtype),
        [
            pltpu.VMEM((4 * count,) + part.shape, part.dtype),
            pltpu.SemaphoreType.DMA(()),
            pltpu.SemaphoreType.DMA(()),
        ],
        6,
        part,
    )


def column_swap(value, over_segment, over_dp):
    pairs = []
    for s in range(2):
        for d in range(2):
            pairs.append((s * 2 + d, (s ^ over_segment) * 2 + (d ^ over_dp)))
    return lax.ppermute(value, ("segment", "dp"), pairs)


SWAPS = ((1, 0), (0, 1), (1, 1))


def slot_matrix(routes, experts, capacity):
    row_count, top_count = routes.shape
    flat_ids = routes.reshape(row_count * top_count)
    onehot = (flat_ids[:, None] == jnp.arange(experts, dtype=jnp.int32)[None, :]).astype(jnp.int32)
    before = jnp.cumsum(onehot, axis=0) - onehot
    slot_rank = jnp.sum(before * onehot, axis=1)
    position = flat_ids * capacity + slot_rank
    columns = jnp.arange(experts * capacity, dtype=jnp.int32)[None, :]
    slot_table = (position[:, None] == columns).astype(BF16)
    return jnp.sum(slot_table.reshape(row_count, top_count, experts * capacity), axis=1)


def mm(a, b, dims):
    return lax.dot_general(a, b, (dims, ((), ())), preferred_element_type=F32)


def body(
    features,
    routes,
    arm_ids,
    targets,
    trunk_gain,
    gate_weight,
    up_weight,
    down_weight,
    tower_in,
    tower_out,
):
    batches, rows_here, width = features.shape
    count = lax.axis_size("expert")
    experts = count
    capacity = max(2, 2 * routes.shape[2] * rows_here // experts)
    towers, _, piece = tower_in.shape
    loss_scale = float(batches * rows_here * count * lax.axis_size("dp")) ** (-0.5)
    seg = lax.axis_index("segment")
    w_gate, w_up, w_down = gate_weight[0], up_weight[0], down_weight[0]

    cols = towers * piece
    extra = jnp.zeros((16, cols), BF16).at[0].set(tower_out.reshape(cols))
    own = jnp.concatenate([tower_in.transpose(1, 0, 2).reshape(width, cols), extra], axis=0)
    pieces = [own] + [column_swap(own, *s) for s in SWAPS]

    wide_rows = features.astype(F32)
    scaled = wide_rows * lax.rsqrt(jnp.mean(wide_rows * wide_rows, axis=-1, keepdims=True) + EPSILON)
    normed = (scaled * trunk_gain).astype(BF16)
    tables = [slot_matrix(routes[b], experts, capacity) for b in range(batches)]
    outgoing = jnp.stack(
        [
            mm(tables[b], normed[b], ((0,), (0,))).astype(BF16).reshape(experts, capacity, width)
            for b in range(batches)
        ],
        axis=1,
    ).reshape(experts, batches * capacity, width)
    own_table = jnp.where(seg == 0, tables[0], tables[1])
    own_arms = jnp.where(seg == 0, arm_ids[0], arm_ids[1])
    own_targets = jnp.where(seg == 0, targets[0], targets[1])
    aux = jnp.concatenate([own_targets, own_arms.astype(F32)])[None, :]
    aux = jnp.broadcast_to(aux, (8, aux.shape[1]))
    inputs, aux_all = dispatch(outgoing, aux)
    inputs = inputs.reshape(-1, width)

    gate_pre = mm(inputs, w_gate, ((1,), (0,)))
    up_pre = mm(inputs, w_up, ((1,), (0,)))
    active = (jax.nn.silu(gate_pre) * up_pre).astype(BF16)
    produced = mm(active, w_down, ((1,), (0,))).astype(BF16)
    returned = giveback(produced.reshape(-1, capacity, width), count)
    table4 = jnp.concatenate([own_table] * 4, axis=1)
    added = mm(table4, returned.reshape(-1, width), ((1,), (0,)))
    own_rows = jnp.where(seg == 0, features[0], features[1])
    mixed = (own_rows.astype(F32) + added).astype(BF16)

    rows = gather(mixed, count).reshape(-1, width)
    packed = jnp.concatenate(pieces, axis=1)
    w_in = packed[:width]
    w_out = packed[width]
    column_tower = lax.rem(jnp.arange(4 * cols, dtype=jnp.int32), cols) // piece
    tower_mask = column_tower[:, None] == jnp.arange(8, dtype=jnp.int32)[None, :]
    out_matrix = jnp.where(tower_mask, w_out[:, None], jnp.zeros((), BF16))
    pre_act = mm(rows, w_in, ((1,), (0,)))
    sig = jax.nn.sigmoid(pre_act)
    hidden = (pre_act * sig).astype(BF16)
    slope = (sig * (1.0 + pre_act * (1.0 - sig))).astype(BF16)
    values = mm(hidden, out_matrix, ((1,), (0,)))
    aux_all = aux_all[:, 0, :].reshape(count // 2, 2, 2 * rows_here)
    aux_all = aux_all.transpose(1, 0, 2).reshape(count, 2, rows_here)
    all_targets = aux_all[:, 0].reshape(-1)
    all_arms = aux_all[:, 1].reshape(-1)
    arm_mask = all_arms[:, None] + 1.0 == jnp.arange(8, dtype=F32)[None, :]
    picked = jnp.sum(jnp.where(arm_mask, values, 0.0), axis=1)
    own_values = jnp.stack([values[:, 0], picked]).astype(BF16).reshape(-1, 128)
    summed = jnp.sum(share(own_values, count).astype(F32), axis=0).reshape(2, -1)
    treated = (all_arms != 0.0).astype(F32)
    grad_first = loss_scale * (jax.nn.sigmoid(summed[0]) - treated)
    grad_arm = loss_scale * (summed[1] - all_targets)
    first_mask = jnp.arange(8, dtype=jnp.int32)[None, :] == 0
    grad_value = jnp.where(first_mask, grad_first[:, None], jnp.where(arm_mask, grad_arm[:, None], 0.0))
    grad_value = grad_value.astype(BF16)
    spread_value = mm(grad_value, out_matrix, ((1,), (1,)))
    grad_pre = (spread_value * slope.astype(F32)).astype(BF16)
    part_rows = mm(grad_pre, w_in, ((1,), (1,))).astype(BF16)
    grad_rows = scatter(part_rows.reshape(count, rows_here, width))

    part_in = mm(rows, grad_pre, ((0,), (0,))).astype(BF16)
    part_out = mm(grad_value, hidden, ((0,), (0,)))
    part_out = jnp.sum(jnp.where(tower_mask.T, part_out, 0.0), axis=0)
    extra = jnp.zeros((16, 4 * cols), BF16).at[0].set(part_out.astype(BF16))
    parts = jnp.concatenate([part_in, extra], axis=0)
    tower_sum = parts[:, :cols].astype(F32)
    for k, s in enumerate(SWAPS):
        sent = parts[:, (k + 1) * cols : (k + 2) * cols]
        tower_sum = tower_sum + column_swap(sent, *s).astype(F32)
    tower_sum = tower_sum.astype(BF16)
    grad_tower_in = tower_sum[:width].reshape(width, towers, piece).transpose(1, 0, 2)
    grad_tower_out = tower_sum[width].reshape(towers, piece)

    back_slots = mm(own_table, grad_rows, ((0,), (0,))).astype(BF16)
    grads = spread(back_slots.reshape(experts, capacity, width)).reshape(-1, width)
    grad_active = mm(grads, w_down, ((1,), (1,)))
    sig = jax.nn.sigmoid(gate_pre)
    grad_gate_pre = (grad_active * up_pre * (sig * (1.0 + gate_pre * (1.0 - sig)))).astype(BF16)
    grad_up_pre = (grad_active * (gate_pre * sig)).astype(BF16)
    sum_gate = mm(inputs, grad_gate_pre, ((0,), (0,)))
    sum_up = mm(inputs, grad_up_pre, ((0,), (0,)))
    sum_down = mm(active, grads, ((0,), (0,)))
    gain_part = jnp.sum(sum_gate * w_gate.astype(F32) + sum_up * w_up.astype(F32), axis=1)
    gain_part = jnp.zeros((8, 128), F32).at[:4].set((gain_part / trunk_gain).reshape(4, 128))
    grad_gain = add_all(gain_part, count)[:4].reshape(width)
    return (
        sum_gate.astype(BF16)[None],
        sum_up.astype(BF16)[None],
        sum_down.astype(BF16)[None],
        grad_tower_in,
        grad_tower_out,
        grad_gain,
    )


def solution(mesh):
    in_specs = (
        P(None, ("expert", "dp"), None),
        P(None, ("expert", "dp"), None),
        P(None, ("expert", "dp")),
        P(None, ("expert", "dp")),
        P(),
        P("expert", None, ("segment", "dp")),
        P("expert", None, ("segment", "dp")),
        P("expert", ("segment", "dp"), None),
        P(None, None, ("segment", "expert", "dp")),
        P(None, ("segment", "expert", "dp")),
    )
    out_specs = (
        P("expert", None, ("segment", "dp")),
        P("expert", None, ("segment", "dp")),
        P("expert", ("segment", "dp"), None),
        P(None, None, ("segment", "expert", "dp")),
        P(None, ("segment", "expert", "dp")),
        P(),
    )
    return jax.shard_map(body, mesh=mesh, in_specs=in_specs, out_specs=out_specs, check_vma=False)
```

```python
import functools

import jax
import jax.numpy as jnp
from jax import lax
from jax.experimental import pallas as pl
from jax.experimental.pallas import tpu as pltpu
from jax.sharding import PartitionSpec as P

EPSILON = 1e-06
MESH = pl.DeviceIdType.MESH
F32 = jnp.float32
BF16 = jnp.bfloat16
NN = (((1,), (0,)), ((), ()))
NT = (((1,), (1,)), ((), ()))
TN = (((0,), (0,)), ((), ()))


def mm(a, b, dims=NN):
    return lax.dot_general(a, b, dims, preferred_element_type=F32)


def wait_bytes(ref, sem):
    pltpu.make_async_copy(ref, ref, sem).wait()


def wide(block):
    depth, rows, width = block.shape
    return block.astype(F32).reshape(depth * rows, width).astype(BF16)


def step_kernel(
    loss_scale,
    feats,
    routes,
    aux,
    gain,
    w_gate,
    w_up,
    w_down,
    own_piece,
    out_gate,
    out_up,
    out_down,
    out_tower,
    out_gain,
    tables,
    outgoing,
    x_in,
    x_rows,
    x_turned,
    by_gate,
    by_up,
    active,
    active_turned,
    p_out,
    r_in,
    mixed,
    mixed_turned,
    aux_in,
    weights,
    hidden,
    slope,
    values,
    value_out,
    value_in,
    grad_turned,
    grad_column,
    d_out,
    d_in,
    b_out,
    g_in,
    g_rows,
    w_pair_out,
    w_pair_in,
    w_z_out,
    w_z_in,
    gain_a_out,
    gain_a_in,
    gain_b_out,
    gain_b_in,
    x_send,
    x_recv,
    aux_send,
    aux_recv,
    p_send,
    p_recv,
    m_send,
    m_recv,
    v_send,
    v_recv,
    d_send,
    d_recv,
    g_send,
    g_recv,
    wz_send,
    wz_recv,
    wp_send,
    wp_recv,
    tp_send,
    tp_recv,
    tz_send,
    tz_recv,
    ga_send,
    ga_recv,
    gb_send,
    gb_recv,
):
    seg, me, dp = lax.axis_index("segment"), lax.axis_index("expert"), lax.axis_index("dp")
    batches, rows_here, width = feats.shape
    count = x_in.shape[0] // 4
    chips = count // 2
    capacity = x_in.shape[1]
    hidden_here = w_gate.shape[1]
    slots = count * capacity
    chip, core = me // 2, lax.rem(me, 2)
    twin = chip * 2 + 1 - core
    z_mine = dp * 2 + seg
    side = 4
    quarter = rows_here * chips // side
    z_peers = {1: (1 - seg, dp), 2: (seg, 1 - dp), 3: (1 - seg, 1 - dp)}

    def remote(src, dst, send, recv, to_seg, expert, to_dp):
        return pltpu.make_async_remote_copy(
            src_ref=src,
            dst_ref=dst,
            send_sem=send,
            recv_sem=recv,
            device_id=(to_seg, expert, to_dp),
            device_id_type=MESH,
        )

    barrier = pltpu.get_barrier_semaphore()

    def greet(i, carry):
        e, z = i // 4, lax.rem(i, 4)
        pl.semaphore_signal(
            barrier,
            inc=1,
            device_id=(
                lax.rem(seg + lax.rem(z, 2), 2),
                lax.rem(me + e, count),
                lax.rem(dp + z // 2, 2),
            ),
            device_id_type=MESH,
        )
        return carry

    lax.fori_loop(1, 4 * count, greet, 0)

    row_ids = lax.broadcasted_iota(jnp.int32, (rows_here, rows_here), 0)
    col_ids = lax.broadcasted_iota(jnp.int32, (rows_here, rows_here), 1)
    lower = (col_ids < row_ids).astype(F32).astype(BF16)
    expert_ids = lax.broadcasted_iota(jnp.int32, (rows_here, count), 1)
    stretch_row = lax.broadcasted_iota(jnp.int32, (count, slots), 0)
    stretch_col = lax.broadcasted_iota(jnp.int32, (count, slots), 1)
    stretch = (stretch_col // capacity == stretch_row).astype(F32).astype(BF16)
    slot_ids = lax.rem(
        lax.broadcasted_iota(jnp.int32, (rows_here, slots), 1), capacity
    ).astype(F32)
    for b in range(batches):
        wide_rows = feats[b].astype(F32)
        scaled = wide_rows * lax.rsqrt(
            jnp.mean(wide_rows * wide_rows, axis=-1, keepdims=True) + EPSILON
        )
        normed = (scaled * gain[...]).astype(BF16)
        named = routes[b]
        taken = jnp.where(
            (named[:, 0:1] == expert_ids) | (named[:, 1:2] == expert_ids), 1.0, 0.0
        ).astype(BF16)
        rank = mm(lower, taken).astype(BF16)
        taken_wide = mm(taken, stretch)
        rank_wide = mm(rank, stretch)
        table = jnp.where((taken_wide > 0.5) & (rank_wide == slot_ids), 1.0, 0.0).astype(BF16)
        tables[b] = table
        outgoing[b] = mm(table, normed, TN).reshape(count, capacity, width).astype(BF16)
    weights[core] = own_piece[...]

    pl.semaphore_wait(barrier, 4 * count - 1)

    def dispatch(i, carry):
        to = lax.rem(me + i, count)
        for b in range(batches):
            mine = (dp * 2 + b) * count + me
            block = outgoing.at[b, to]
            remote(block, x_in.at[mine], x_send, x_recv.at[1], 1 - seg, to, 1 - dp).start()

            @pl.when(i > 0)
            def _():
                remote(block, x_in.at[mine], x_send, x_recv.at[0], seg, to, dp).start()

        return carry

    lax.fori_loop(0, count, dispatch, 0)
    for b in range(batches):
        pltpu.make_async_copy(
            outgoing.at[b, me], x_in.at[(dp * 2 + b) * count + me], x_recv.at[0]
        ).start()

    def send_weights(k):
        to_seg, to_dp = z_peers[k]
        remote(
            own_piece, weights.at[k * 2 + core], wz_send.at[k], wz_recv.at[k], to_seg, me, to_dp
        ).start()

    def relay_weights(k):
        block = weights.at[k * 2 + core]
        wait_bytes(block, wz_recv.at[k])
        remote(block, block, wp_send.at[k], wp_recv.at[k], seg, twin, dp).start()

    remote(own_piece, weights.at[core], wp_send.at[0], wp_recv.at[0], seg, twin, dp).start()
    send_weights(1)

    def send_aux(i, carry):
        to = lax.rem(chip + i, chips)
        remote(aux, aux_in.at[chip], aux_send, aux_recv, seg, to * 2 + core, dp).start()
        return carry

    lax.fori_loop(1, chips, send_aux, 0)
    aux_in[chip] = aux[...]

    def forward(j, carry):
        to_dp = lax.rem(dp + j // 2, 2)
        to_seg = lax.rem(j, 2)
        base = (to_dp * 2 + to_seg) * count

        @pl.when(j == 0)
        def _():
            wait_bytes(x_in.at[pl.ds(dp * 2 * count, 2 * count)], x_recv.at[0])

        @pl.when(j == 2)
        def _():
            wait_bytes(x_in.at[pl.ds((1 - dp) * 2 * count, 2 * count)], x_recv.at[1])

        here = pl.ds(pl.multiple_of(base * capacity, slots), slots)
        rows = wide(x_in[pl.ds(base, count)])
        x_rows[here] = rows
        gate_pre = mm(rows, w_gate[...])
        up_pre = mm(rows, w_up[...])
        sig = jax.nn.sigmoid(gate_pre)
        gated = gate_pre * sig
        act = (gated * up_pre).astype(BF16)
        by_up[here] = gated.astype(BF16)
        by_gate[here] = (up_pre * (sig * (1.0 + gate_pre * (1.0 - sig)))).astype(BF16)
        active[here] = act
        made = mm(act, w_down[...])
        p_out[pl.ds(base, count)] = made.reshape(count, capacity, width).astype(BF16)
        local = (to_dp == dp) & (to_seg == seg)

        def give(i, inner):
            e = lax.rem(me + i, count)

            @pl.when((i > 0) | jnp.logical_not(local))
            def _():
                remote(
                    p_out.at[base + e],
                    r_in.at[z_mine * count + me],
                    p_send,
                    p_recv,
                    to_seg,
                    e,
                    to_dp,
                ).start()

            return inner

        lax.fori_loop(0, count, give, 0)

        @pl.when(local)
        def _():
            pltpu.make_async_copy(
                p_out.at[base + me], r_in.at[z_mine * count + me], p_recv
            ).start()

        return carry

    lax.fori_loop(0, 4, forward, 0)
    relay_weights(1)

    def turn(j, carry):
        here = pl.ds(pl.multiple_of(j * slots, slots), slots)
        x_turned[:, here] = x_rows[here].T
        active_turned[:, here] = active[here].T
        return carry

    lax.fori_loop(0, 4, turn, 0)

    wait_bytes(r_in, p_recv)
    own_table = tables[seg]
    added = mm(own_table, wide(r_in[pl.ds(0, count)]))
    for z in range(1, 4):
        added = added + mm(own_table, wide(r_in[pl.ds(z * count, count)]))
    mixed[chip] = (feats[seg].astype(F32) + added).astype(BF16)

    def send_rows(i, carry):
        to = lax.rem(chip + i, chips)
        block = mixed.at[chip]
        remote(block, block, m_send, m_recv.at[chip // side], seg, to * 2 + core, dp).start()
        return carry

    lax.fori_loop(1, chips, send_rows, 0)
    send_weights(3)
    send_weights(2)

    depth = width
    tower_count = 8
    out_cols = own_piece.shape[1]
    per_tower = out_cols // tower_count
    mask_tower = lax.broadcasted_iota(jnp.int32, (16, out_cols), 0)
    mask_col = lax.broadcasted_iota(jnp.int32, (16, out_cols), 1) // per_tower
    tower_mask = mask_tower == mask_col

    def out_matrix(piece):
        tail = weights[piece, depth:, :].astype(F32)
        return jnp.where(tower_mask, tail[0:1, :], 0.0).astype(BF16)

    def tower_forward(piece, group, fresh):
        here = pl.ds(pl.multiple_of(group * quarter, quarter), quarter)
        blocks = mixed[pl.ds(group * side, side)]
        rows = blocks.reshape(quarter, width)
        pre_act = mm(rows, weights[piece, :depth, :])
        sig = jax.nn.sigmoid(pre_act)
        hid = (pre_act * sig).astype(BF16)
        hidden[piece, here] = hid
        slope[piece, here] = (sig * (1.0 + pre_act * (1.0 - sig))).astype(BF16)
        part = mm(out_matrix(piece), hid, NT)
        if fresh:
            values[:, here] = part
        else:
            values[:, here] += part

    wait_bytes(weights.at[0], wp_recv.at[0])
    for j, ahead in enumerate((0, 1, 3, 2)):
        group = lax.rem(chip // side + ahead, side)
        if ahead == 0:
            wait_bytes(mixed.at[pl.ds(0, side - 1)], m_recv.at[group])
        else:
            wait_bytes(mixed.at[pl.ds(0, side)], m_recv.at[group])
        if j == 0:
            wait_bytes(weights.at[0], wp_recv.at[1])
        tower_forward(0, group, True)

        def more(p, carry, group=group):
            tower_forward(p, group, False)
            return carry

        lax.fori_loop(1, 4, more, 0)
    for k in (3, 2):
        relay_weights(k)
        for turn_core in (core, 1 - core):
            if turn_core is not core:
                wait_bytes(weights.at[0], wp_recv.at[k])

            def more_groups(group, carry, piece=k * 2 + turn_core):
                tower_forward(piece, group, False)
                return carry

            lax.fori_loop(0, side, more_groups, 0)

    wait_bytes(aux_in.at[pl.ds(0, chips - 1)], aux_recv)
    pairs = [aux_in[2 * g] + aux_in[2 * g + 1] for g in range(chips // 2)]
    notes = jnp.concatenate(pairs, axis=1)
    all_targets, all_arms = notes[0:1], notes[1:2]
    all_rows = chips * rows_here
    tower_ids = lax.broadcasted_iota(jnp.int32, (16, all_rows), 0).astype(F32)
    arm_mask = tower_ids - 1.0 == all_arms
    every = values[...]
    value_out[0:1] = every[0:1]
    value_out[1:2] = jnp.sum(jnp.where(arm_mask, every, 0.0), axis=0, keepdims=True)

    def send_values(i, carry):
        to = lax.rem(chip + i, chips)
        remote(value_out, value_in.at[chip], v_send, v_recv, seg, to * 2 + core, dp).start()
        return carry

    lax.fori_loop(1, chips, send_values, 0)
    value_in[chip] = value_out[...]
    for g in range(side):
        mixed_turned[:, g * quarter : (g + 1) * quarter] = (
            mixed[g * side : (g + 1) * side].reshape(quarter, width).T
        )
    wait_bytes(value_in.at[pl.ds(0, chips - 1)], v_recv)
    summed = value_in[0]
    for i in range(1, chips):
        summed = summed + value_in[i]
    treated = jnp.where(all_arms != 0.0, 1.0, 0.0)
    grad_first = loss_scale * (jax.nn.sigmoid(summed[0:1]) - treated)
    grad_arm = loss_scale * (summed[1:2] - all_targets)
    grad_value = jnp.where(tower_ids == 0.0, grad_first, jnp.where(arm_mask, grad_arm, 0.0))
    grad_turned[...] = grad_value.astype(BF16)
    grad_column[...] = grad_value.T.astype(BF16)

    def tower_back(j, carry):
        group = lax.rem(chip // side + 2 + j, side)
        here = pl.ds(pl.multiple_of(group * quarter, quarter), quarter)

        def one(p, total):
            spread_value = mm(grad_column[here], out_matrix(p))
            grad_pre = (spread_value * slope[p, here].astype(F32)).astype(BF16)
            slope[p, here] = grad_pre
            return total + mm(grad_pre, weights[p, :depth, :], NT)

        def two(p, total):
            return one(2 * p + 1, one(2 * p, total))

        total = lax.fori_loop(0, 4, two, jnp.zeros((quarter, width), F32))
        d_out[pl.ds(group * side, side)] = total.astype(BF16).reshape(side, rows_here, width)

        def send_grads(i, inner):
            to = group * side + i

            @pl.when(to != chip)
            def _():
                remote(
                    d_out.at[to], d_in.at[chip], d_send, d_recv, seg, to * 2 + core, dp
                ).start()

            return inner

        lax.fori_loop(0, side, send_grads, 0)
        return carry

    lax.fori_loop(0, side, tower_back, 0)
    d_in[chip] = d_out[chip]

    def tower_weight_grad(piece):
        main = mm(mixed_turned[...], slope[piece])
        tail = mm(grad_turned[...], hidden[piece])
        tail = jnp.sum(jnp.where(tower_mask, tail, 0.0), axis=0, keepdims=True)
        tail = jnp.where(mask_tower == 0, tail, 0.0)
        return main, tail

    def twin_grads(i, carry):
        k = 3 - i
        main, tail = tower_weight_grad(k * 2 + 1 - core)
        w_pair_out[k, :depth, :] = main.astype(BF16)
        w_pair_out[k, depth:, :] = tail.astype(BF16)
        remote(
            w_pair_out.at[k], w_pair_in.at[k], tp_send, tp_recv.at[k], seg, twin, dp
        ).start()
        return carry

    lax.fori_loop(0, 4, twin_grads, 0)

    wait_bytes(d_in.at[pl.ds(0, chips - 1)], d_recv)
    total = d_in[0].astype(F32)
    for i in range(1, chips):
        total = total + d_in[i].astype(F32)
    b_out[...] = mm(own_table, total.astype(BF16), TN).reshape(count, capacity, width).astype(BF16)

    def spread(i, carry):
        e, z = lax.rem(me + i // 4, count), lax.rem(i, 4)
        to_seg, to_dp = lax.rem(seg + lax.rem(z, 2), 2), lax.rem(dp + z // 2, 2)
        remote(
            b_out.at[e], g_in.at[z_mine * count + me], g_send, g_recv.at[z_mine], to_seg, e, to_dp
        ).start()
        return carry

    lax.fori_loop(1, 4 * count, spread, 0)
    pltpu.make_async_copy(b_out.at[me], g_in.at[z_mine * count + me], g_recv.at[z_mine]).start()

    for k in (3, 2, 1, 0):
        main, tail = tower_weight_grad(k * 2 + core)
        wait_bytes(w_pair_in.at[k], tp_recv.at[k])
        main = main + w_pair_in[k, :depth, :].astype(F32)
        tail = tail + w_pair_in[k, depth:, :].astype(F32)
        w_z_out[k, :depth, :] = main.astype(BF16)
        w_z_out[k, depth:, :] = tail.astype(BF16)
        if k:
            to_seg, to_dp = z_peers[k]
            remote(
                w_z_out.at[k], w_z_in.at[k], tz_send.at[k], tz_recv.at[k], to_seg, me, to_dp
            ).start()

    def backward(j, carry):
        z = lax.rem(z_mine + j, 4)
        wait_bytes(g_in.at[pl.ds(z * count, count)], g_recv.at[z])
        here = pl.ds(pl.multiple_of(z * slots, slots), slots)
        grads = wide(g_in[pl.ds(z * count, count)])
        g_rows[here] = grads
        grad_active = mm(grads, w_down[...], NT)
        by_gate[here] = (grad_active * by_gate[here].astype(F32)).astype(BF16)
        by_up[here] = (grad_active * by_up[here].astype(F32)).astype(BF16)
        return carry

    lax.fori_loop(0, 4, backward, 0)
    strip = 256

    def gate_grads(j, total):
        cols = pl.ds(pl.multiple_of(j * strip, strip), strip)
        for source, weight, out in ((by_gate, w_gate, out_gate), (by_up, w_up, out_up)):
            grad = mm(x_turned[...], source[:, cols])
            out[:, cols] = grad.astype(BF16)
            term = grad * weight[:, cols].astype(F32)
            for c in range(strip // 128):
                total = total + term[:, c * 128 : (c + 1) * 128]
        return total

    gain_sum = lax.fori_loop(0, hidden_here // strip, gate_grads, jnp.zeros((width, 128), F32))
    gain_row = jnp.sum(gain_sum.T, axis=0, keepdims=True)
    gain_a_out[...] = gain_row / gain[...]
    mine_a = z_mine * 2 + core
    others = []
    for flip_seg in range(2):
        for flip_dp in range(2):
            for flip_core in range(2):
                if flip_seg or flip_dp or flip_core:
                    others.append((flip_seg, flip_dp, flip_core))
    for flip_seg, flip_dp, flip_core in others:
        remote(
            gain_a_out,
            gain_a_in.at[mine_a],
            ga_send,
            ga_recv,
            1 - seg if flip_seg else seg,
            twin if flip_core else me,
            1 - dp if flip_dp else dp,
        ).start()
    gain_a_in[mine_a] = gain_a_out[...]

    def down_grads(j, carry):
        here = pl.ds(pl.multiple_of(j * strip, strip), strip)
        out_down[here] = mm(active_turned[here], g_rows[...]).astype(BF16)
        return carry

    half = hidden_here // strip // 2
    lax.fori_loop(0, half, down_grads, 0)
    wait_bytes(gain_a_in.at[pl.ds(0, 7)], ga_recv)
    part = gain_a_in[0]
    for i in range(1, 8):
        part = part + gain_a_in[i]
    gain_b_out[...] = part

    def send_gain(i, carry):
        to = lax.rem(chip + i, chips)
        remote(gain_b_out, gain_b_in.at[chip], gb_send, gb_recv, seg, to * 2 + core, dp).start()
        return carry

    lax.fori_loop(1, chips, send_gain, 0)
    gain_b_in[chip] = gain_b_out[...]
    lax.fori_loop(half, hidden_here // strip, down_grads, 0)

    tower_sum = w_z_out[0].astype(F32)
    for k in (1, 3, 2):
        wait_bytes(w_z_in.at[k], tz_recv.at[k])
        tower_sum = tower_sum + w_z_in[k].astype(F32)
    out_tower[...] = tower_sum.astype(BF16)
    wait_bytes(gain_b_in.at[pl.ds(0, chips - 1)], gb_recv)
    part = gain_b_in[0]
    for i in range(1, chips):
        part = part + gain_b_in[i]
    out_gain[...] = part

    wait_bytes(x_in.at[pl.ds(0, 4 * count - 2)], x_send)
    wait_bytes(aux_in.at[pl.ds(0, chips - 1)], aux_send)
    wait_bytes(r_in.at[pl.ds(0, 4 * count - 1)], p_send)
    wait_bytes(mixed.at[pl.ds(0, chips - 1)], m_send)
    wait_bytes(value_in.at[pl.ds(0, chips - 1)], v_send)
    wait_bytes(d_in.at[pl.ds(0, chips - 1)], d_send)
    wait_bytes(g_in.at[pl.ds(0, 4 * count - 1)], g_send)
    for k in range(1, 4):
        wait_bytes(own_piece, wz_send.at[k])
        wait_bytes(own_piece, tz_send.at[k])
    for k in range(4):
        wait_bytes(own_piece, wp_send.at[k])
    wait_bytes(w_pair_in, tp_send)
    wait_bytes(gain_a_in.at[pl.ds(0, 7)], ga_send)
    wait_bytes(gain_b_in.at[pl.ds(0, chips - 1)], gb_send)


def run_step(loss_scale, count, capacity, feats, routes, aux, gain, w_gate, w_up, w_down, piece):
    batches, rows_here, width = feats.shape
    hidden_here = w_gate.shape[1]
    chips = count // 2
    blocks = 4 * count
    slots = blocks * capacity
    all_rows = chips * rows_here
    cols = piece.shape[1]
    v = pltpu.VMEM
    dma = pltpu.SemaphoreType.DMA
    scratch = [
        v((batches, rows_here, count * capacity), BF16),
        v((batches, count, capacity, width), BF16),
        v((blocks, capacity, width), BF16),
        v((slots, width), BF16),
        v((width, slots), BF16),
        v((slots, hidden_here), BF16),
        v((slots, hidden_here), BF16),
        v((slots, hidden_here), BF16),
        v((hidden_here, slots), BF16),
        v((blocks, capacity, width), BF16),
        v((blocks, capacity, width), BF16),
        v((chips, rows_here, width), BF16),
        v((width, all_rows), BF16),
        v((chips, 8, 128), F32),
        v((8,) + piece.shape, BF16),
        v((8, all_rows, cols), BF16),
        v((8, all_rows, cols), BF16),
        v((16, all_rows), F32),
        v((2, all_rows), F32),
        v((chips, 2, all_rows), F32),
        v((16, all_rows), BF16),
        v((all_rows, 16), BF16),
        v((chips, rows_here, width), BF16),
        v((chips, rows_here, width), BF16),
        v((count, capacity, width), BF16),
        v((blocks, capacity, width), BF16),
        v((slots, width), BF16),
        v((4,) + piece.shape, BF16),
        v((4,) + piece.shape, BF16),
        v((4,) + piece.shape, BF16),
        v((4,) + piece.shape, BF16),
        v((1, width), F32),
        v((8, 1, width), F32),
        v((1, width), F32),
        v((chips, 1, width), F32),
        dma(()),
        dma((2,)),
        dma(()),
        dma(()),
        dma(()),
        dma(()),
        dma(()),
        dma((4,)),
        dma(()),
        dma(()),
        dma(()),
        dma(()),
        dma(()),
        dma((4,)),
        dma((4,)),
        dma((4,)),
        dma((4,)),
        dma((4,)),
        dma(()),
        dma((4,)),
        dma((4,)),
        dma((4,)),
        dma(()),
        dma(()),
        dma(()),
        dma(()),
    ]
    out_shape = (
        jax.ShapeDtypeStruct(w_gate.shape, BF16),
        jax.ShapeDtypeStruct(w_up.shape, BF16),
        jax.ShapeDtypeStruct(w_down.shape, BF16),
        jax.ShapeDtypeStruct(piece.shape, BF16),
        jax.ShapeDtypeStruct((1, width), F32),
    )
    spec = pl.BlockSpec(memory_space=pltpu.VMEM)
    return pl.pallas_call(
        functools.partial(step_kernel, loss_scale),
        out_shape=out_shape,
        in_specs=[spec] * 8,
        out_specs=(spec,) * 5,
        scratch_shapes=scratch,
        compiler_params=pltpu.CompilerParams(
            collective_id=0, has_side_effects=True, vmem_limit_bytes=67043328
        ),
    )(feats, routes, aux, gain, w_gate, w_up, w_down, piece)


def body(
    features,
    routes,
    arm_ids,
    targets,
    trunk_gain,
    gate_weight,
    up_weight,
    down_weight,
    tower_in,
    tower_out,
):
    batches, rows_here, width = features.shape
    count = lax.axis_size("expert")
    capacity = max(2, 2 * routes.shape[2] * rows_here // count)
    towers, _, piece = tower_in.shape
    loss_scale = float(batches * rows_here * count * lax.axis_size("dp")) ** (-0.5)
    seg = lax.axis_index("segment")
    odd = lax.rem(lax.axis_index("expert") // 2, 2)
    cols = 8 * piece
    turned = tower_in.transpose(1, 0, 2).reshape(width, towers * piece)
    own = jnp.zeros((width + 16, cols), BF16)
    own = own.at[:width, : towers * piece].set(turned)
    own = own.at[width, : towers * piece].set(tower_out.reshape(towers * piece))
    notes = jnp.stack(
        [
            jnp.where(seg == 0, targets[0], targets[1]),
            jnp.where(seg == 0, arm_ids[0], arm_ids[1]).astype(F32),
        ]
    )
    blank = jnp.zeros_like(notes)
    aux = jnp.concatenate(
        [jnp.where(odd == 0, notes, blank), jnp.where(odd == 0, blank, notes)], axis=1
    )
    aux = jnp.concatenate([aux, jnp.zeros((6, 2 * rows_here), F32)], axis=0)
    grad_gate, grad_up, grad_down, grad_tower, grad_gain = run_step(
        loss_scale,
        count,
        capacity,
        features,
        routes,
        aux,
        trunk_gain.reshape(1, width),
        gate_weight[0],
        up_weight[0],
        down_weight[0],
        own,
    )
    grad_tower_in = grad_tower[:width, : towers * piece].reshape(width, towers, piece)
    return (
        grad_gate[None],
        grad_up[None],
        grad_down[None],
        grad_tower_in.transpose(1, 0, 2),
        grad_tower[width, : towers * piece].reshape(towers, piece),
        grad_gain.reshape(width),
    )


def solution(mesh):
    in_specs = (
        P(None, ("expert", "dp"), None),
        P(None, ("expert", "dp"), None),
        P(None, ("expert", "dp")),
        P(None, ("expert", "dp")),
        P(),
        P("expert", None, ("segment", "dp")),
        P("expert", None, ("segment", "dp")),
        P("expert", ("segment", "dp"), None),
        P(None, None, ("segment", "expert", "dp")),
        P(None, ("segment", "expert", "dp")),
    )
    out_specs = (
        P("expert", None, ("segment", "dp")),
        P("expert", None, ("segment", "dp")),
        P("expert", ("segment", "dp"), None),
        P(None, None, ("segment", "expert", "dp")),
        P(None, ("segment", "expert", "dp")),
        P(),
    )
    return jax.shard_map(body, mesh=mesh, in_specs=in_specs, out_specs=out_specs, check_vma=False)
```

```python
import functools

import jax
import jax.numpy as jnp
from jax import lax
from jax.experimental import pallas as pl
from jax.experimental.pallas import tpu as pltpu
from jax.sharding import PartitionSpec as P

EPSILON = 1e-06
MESH = pl.DeviceIdType.MESH
F32 = jnp.float32
BF16 = jnp.bfloat16
NN = (((1,), (0,)), ((), ()))
NT = (((1,), (1,)), ((), ()))
TN = (((0,), (0,)), ((), ()))


def mm(a, b, dims=NN):
    return lax.dot_general(a, b, dims, preferred_element_type=F32)


def wait_bytes(ref, sem):
    pltpu.make_async_copy(ref, ref, sem).wait()


def sigmoid(value):
    return 0.5 * jnp.tanh(0.5 * value) + 0.5


def wide(block):
    depth, rows, width = block.shape
    return block.astype(F32).reshape(depth * rows, width).astype(BF16)


def step_kernel(
    loss_scale,
    feats,
    routes,
    arms,
    targets,
    gain,
    w_gate,
    w_up,
    w_down,
    tower_in,
    tower_out,
    out_gate,
    out_up,
    out_down,
    out_tower,
    out_tower_row,
    out_gain,
    aux,
    own_piece,
    tail_row,
    sum_row,
    grad_wide,
    tables,
    outgoing,
    x_in,
    x_turned,
    by_gate,
    by_up,
    active_turned,
    p_out,
    r_in,
    mixed,
    mixed_turned,
    aux_in,
    weights,
    hidden,
    slope,
    values,
    value_out,
    value_in,
    grad_turned,
    grad_column,
    d_out,
    d_in,
    b_out,
    g_in,
    g_rows,
    w_pair_out,
    w_pair_in,
    w_z_out,
    w_z_in,
    gain_a_out,
    gain_a_in,
    gain_b_out,
    gain_b_in,
    x_send,
    x_recv,
    aux_send,
    aux_recv,
    p_send,
    p_recv,
    m_send,
    m_recv,
    v_send,
    v_recv,
    d_send,
    d_recv,
    g_send,
    g_recv,
    wz_send,
    wz_recv,
    wp_send,
    wp_recv,
    tp_send,
    tp_recv,
    tz_send,
    tz_recv,
    ga_send,
    ga_recv,
    gb_send,
    gb_recv,
):
    seg, me, dp = lax.axis_index("segment"), lax.axis_index("expert"), lax.axis_index("dp")
    batches, rows_here, width = feats.shape
    count = x_in.shape[0] // 4
    chips = count // 2
    capacity = x_in.shape[1]
    w_gate, w_up, w_down = w_gate.at[0], w_up.at[0], w_down.at[0]
    out_gate, out_up, out_down = out_gate.at[0], out_up.at[0], out_down.at[0]
    hidden_here = w_gate.shape[1]
    towers, _, per_tower = tower_in.shape
    slots = count * capacity
    chip, core = me // 2, lax.rem(me, 2)
    twin = chip * 2 + 1 - core
    z_mine = dp * 2 + seg
    side = 4
    quarter = rows_here * chips // side
    z_peers = {1: (1 - seg, dp), 2: (seg, 1 - dp), 3: (1 - seg, 1 - dp)}

    def remote(src, dst, send, recv, to_seg, expert, to_dp):
        return pltpu.make_async_remote_copy(
            src_ref=src,
            dst_ref=dst,
            send_sem=send,
            recv_sem=recv,
            device_id=(to_seg, expert, to_dp),
            device_id_type=MESH,
        )

    barrier = pltpu.get_barrier_semaphore()

    def greet(i, carry):
        e, z = i // 4, lax.rem(i, 4)
        pl.semaphore_signal(
            barrier,
            inc=1,
            device_id=(
                lax.rem(seg + lax.rem(z, 2), 2),
                lax.rem(me + e, count),
                lax.rem(dp + z // 2, 2),
            ),
            device_id_type=MESH,
        )
        return carry

    lax.fori_loop(1, 4 * count, greet, 0, unroll=8)

    row_ids = lax.broadcasted_iota(jnp.int32, (rows_here, rows_here), 0)
    col_ids = lax.broadcasted_iota(jnp.int32, (rows_here, rows_here), 1)
    lower = (col_ids < row_ids).astype(F32).astype(BF16)
    expert_ids = lax.broadcasted_iota(jnp.int32, (rows_here, count), 1)
    stretch_row = lax.broadcasted_iota(jnp.int32, (count, slots), 0)
    stretch_col = lax.broadcasted_iota(jnp.int32, (count, slots), 1)
    stretch = (stretch_col // capacity == stretch_row).astype(F32).astype(BF16)
    slot_ids = lax.rem(
        lax.broadcasted_iota(jnp.int32, (rows_here, slots), 1), capacity
    ).astype(F32)
    for b in range(batches):
        wide_rows = feats[b].astype(F32)
        scaled = wide_rows * lax.rsqrt(
            jnp.mean(wide_rows * wide_rows, axis=-1, keepdims=True) + EPSILON
        )
        normed = (scaled * gain[...]).astype(BF16)
        named = routes[b]
        taken = jnp.where(
            (named[:, 0:1] == expert_ids) | (named[:, 1:2] == expert_ids), 1.0, 0.0
        ).astype(BF16)
        rank = mm(lower, taken).astype(BF16)
        taken_wide = mm(taken, stretch)
        rank_wide = mm(rank, stretch)
        table = jnp.where((taken_wide > 0.5) & (rank_wide == slot_ids), 1.0, 0.0).astype(BF16)
        tables[b] = table
        outgoing[b] = mm(table, normed, TN).reshape(count, capacity, width).astype(BF16)
    own_piece[...] = jnp.zeros_like(own_piece)
    tail_row[...] = jnp.zeros_like(tail_row)
    for t in range(towers):
        here = slice(t * per_tower, (t + 1) * per_tower)
        own_piece[:width, here] = tower_in[t]
        tail_row[0:1, here] = tower_out[t : t + 1, :].astype(F32)
    own_piece[width:, :] = tail_row[...].astype(BF16)
    weights[core] = own_piece[...]
    aux[...] = jnp.zeros_like(aux)
    own_targets = jnp.where(seg == 0, targets[0:1, :], targets[1:2, :])
    own_arms = jnp.where(seg == 0, arms[0:1, :], arms[1:2, :]).astype(F32)
    for odd in range(2):

        @pl.when(lax.rem(chip, 2) == odd)
        def _():
            aux[0:1, odd * rows_here : (odd + 1) * rows_here] = own_targets
            aux[1:2, odd * rows_here : (odd + 1) * rows_here] = own_arms


    pl.semaphore_wait(barrier, 4 * count - 1)

    def dispatch(i, carry):
        to = lax.rem(me + i, count)
        for b in range(batches):
            mine = (dp * 2 + b) * count + me
            block = outgoing.at[b, to]
            remote(block, x_in.at[mine], x_send, x_recv.at[1], 1 - seg, to, 1 - dp).start()

            @pl.when(i > 0)
            def _():
                remote(block, x_in.at[mine], x_send, x_recv.at[0], seg, to, dp).start()

        return carry

    lax.fori_loop(0, count, dispatch, 0)
    for b in range(batches):
        pltpu.make_async_copy(
            outgoing.at[b, me], x_in.at[(dp * 2 + b) * count + me], x_recv.at[0]
        ).start()

    def send_weights(k):
        to_seg, to_dp = z_peers[k]
        remote(
            own_piece, weights.at[k * 2 + core], wz_send.at[k], wz_recv.at[k], to_seg, me, to_dp
        ).start()

    def relay_weights(k):
        block = weights.at[k * 2 + core]
        wait_bytes(block, wz_recv.at[k])
        remote(block, block, wp_send.at[k], wp_recv.at[k], seg, twin, dp).start()

    remote(own_piece, weights.at[core], wp_send.at[0], wp_recv.at[0], seg, twin, dp).start()
    send_weights(1)

    def send_aux(i, carry):
        to = lax.rem(chip + i, chips)
        remote(aux, aux_in.at[chip], aux_send, aux_recv, seg, to * 2 + core, dp).start()
        return carry

    lax.fori_loop(1, chips, send_aux, 0)
    aux_in[chip] = aux[...]

    def forward(j, carry):
        to_dp = lax.rem(dp + j // 2, 2)
        to_seg = lax.rem(j, 2)
        base = (to_dp * 2 + to_seg) * count

        @pl.when(j == 0)
        def _():
            wait_bytes(x_in.at[pl.ds(dp * 2 * count, 2 * count)], x_recv.at[0])

        @pl.when(j == 2)
        def _():
            wait_bytes(x_in.at[pl.ds((1 - dp) * 2 * count, 2 * count)], x_recv.at[1])

        here = pl.ds(pl.multiple_of(base * capacity, slots), slots)
        rows = wide(x_in[pl.ds(base, count)])
        gate_pre = mm(rows, w_gate[...])
        up_pre = mm(rows, w_up[...])
        sig = sigmoid(gate_pre)
        gated = gate_pre * sig
        act = (gated * up_pre).astype(BF16)
        by_up[here] = gated.astype(BF16)
        by_gate[here] = (up_pre * (sig + gated - gated * sig)).astype(BF16)
        half_hidden = hidden_here // 2
        hidden[0, here] = act[:, :half_hidden]
        hidden[1, here] = act[:, half_hidden:]
        made = mm(act, w_down[...])
        p_out[pl.ds(base, count)] = made.reshape(count, capacity, width).astype(BF16)
        local = (to_dp == dp) & (to_seg == seg)

        def give(i, inner):
            e = lax.rem(me + i, count)

            @pl.when((i > 0) | jnp.logical_not(local))
            def _():
                remote(
                    p_out.at[base + e],
                    r_in.at[z_mine * count + me],
                    p_send,
                    p_recv,
                    to_seg,
                    e,
                    to_dp,
                ).start()

            return inner

        lax.fori_loop(0, count, give, 0)

        @pl.when(local)
        def _():
            pltpu.make_async_copy(
                p_out.at[base + me], r_in.at[z_mine * count + me], p_recv
            ).start()

        return carry

    lax.fori_loop(0, 4, forward, 0)
    send_weights(3)
    relay_weights(1)

    def turn(j, carry):
        here = pl.ds(pl.multiple_of(j * slots, slots), slots)
        x_turned[:, here] = wide(x_in[pl.ds(j * count, count)]).T
        active_turned[: hidden_here // 2, here] = hidden[0, here].T
        active_turned[hidden_here // 2 :, here] = hidden[1, here].T
        return carry

    lax.fori_loop(0, 4, turn, 0)

    wait_bytes(r_in, p_recv)
    own_table = tables[seg]
    added = mm(own_table, wide(r_in[pl.ds(0, count)]))
    for z in range(1, 4):
        added = added + mm(own_table, wide(r_in[pl.ds(z * count, count)]))
    mixed[chip] = (feats[seg].astype(F32) + added).astype(BF16)

    def send_rows(i, carry):
        to = lax.rem(chip + i, chips)
        block = mixed.at[chip]
        remote(block, block, m_send, m_recv.at[chip // side], seg, to * 2 + core, dp).start()
        return carry

    lax.fori_loop(1, chips, send_rows, 0)

    depth = width
    out_cols = own_piece.shape[1]
    mask_tower = lax.broadcasted_iota(jnp.int32, (16, out_cols), 0)
    mask_col = lax.broadcasted_iota(jnp.int32, (16, out_cols), 1) // per_tower
    tower_mask = mask_tower == mask_col

    def out_matrix(piece):
        tail = weights[piece, depth:, :].astype(F32)
        return jnp.where(tower_mask, tail[0:1, :], 0.0).astype(BF16)

    def tower_forward(piece, group, fresh):
        here = pl.ds(pl.multiple_of(group * quarter, quarter), quarter)
        blocks = mixed[pl.ds(group * side, side)]
        rows = blocks.reshape(quarter, width)
        pre_act = mm(rows, weights[piece, :depth, :])
        sig = sigmoid(pre_act)
        hid_wide = pre_act * sig
        hid = hid_wide.astype(BF16)
        hidden[piece, here] = hid
        tail = weights[piece, depth:, :].astype(F32)[0:1, :]
        slope[piece, here] = ((sig + hid_wide - hid_wide * sig) * tail).astype(BF16)
        part = mm(out_matrix(piece), hid, NT)
        if fresh:
            values[:, here] = part
        else:
            values[:, here] += part

    wait_bytes(weights.at[0], wp_recv.at[0])
    for j, ahead in enumerate((0, 1, 3, 2)):
        group = lax.rem(chip // side + ahead, side)
        if ahead == 0:
            wait_bytes(mixed.at[pl.ds(0, side - 1)], m_recv.at[group])
        else:
            wait_bytes(mixed.at[pl.ds(0, side)], m_recv.at[group])
        if j == 0:
            wait_bytes(weights.at[0], wp_recv.at[1])
        tower_forward(0, group, True)

        def more(p, carry, group=group):
            tower_forward(p, group, False)
            return carry

        lax.fori_loop(1, 4, more, 0)
        if j == 0:
            relay_weights(3)
            remote(
                weights.at[6 + core],
                weights.at[4 + core],
                wz_send.at[2],
                wz_recv.at[2],
                1 - seg,
                me,
                dp,
            ).start()
    for k in (3, 2):
        if k == 2:
            relay_weights(2)
        for turn_core in (core, 1 - core):
            if turn_core is not core:
                wait_bytes(weights.at[0], wp_recv.at[k])

            def more_groups(group, carry, piece=k * 2 + turn_core):
                tower_forward(piece, group, False)
                return carry

            lax.fori_loop(0, side, more_groups, 0)

    wait_bytes(aux_in.at[pl.ds(0, chips - 1)], aux_recv)
    pairs = [aux_in[2 * g] + aux_in[2 * g + 1] for g in range(chips // 2)]
    notes = jnp.concatenate(pairs, axis=1)
    all_targets, all_arms = notes[0:1], notes[1:2]
    all_rows = chips * rows_here
    tower_ids = lax.broadcasted_iota(jnp.int32, (16, all_rows), 0).astype(F32)
    arm_mask = tower_ids - 1.0 == all_arms
    every = values[...]
    value_out[0:1] = every[0:1]
    value_out[1:2] = jnp.sum(jnp.where(arm_mask, every, 0.0), axis=0, keepdims=True)

    def send_values(i, carry):
        to = lax.rem(chip + i, chips)
        remote(value_out, value_in.at[chip], v_send, v_recv, seg, to * 2 + core, dp).start()
        return carry

    lax.fori_loop(1, chips, send_values, 0)
    value_in[chip] = value_out[...]
    for g in range(side):
        mixed_turned[:, g * quarter : (g + 1) * quarter] = (
            mixed[g * side : (g + 1) * side].reshape(quarter, width).T
        )
    wait_bytes(value_in.at[pl.ds(0, chips - 1)], v_recv)
    summed = value_in[0]
    for i in range(1, chips):
        summed = summed + value_in[i]
    treated = jnp.where(all_arms != 0.0, 1.0, 0.0)
    grad_first = loss_scale * (sigmoid(summed[0:1]) - treated)
    grad_arm = loss_scale * (summed[1:2] - all_targets)
    grad_value = jnp.where(tower_ids == 0.0, grad_first, jnp.where(arm_mask, grad_arm, 0.0))
    grad_turned[...] = grad_value.astype(BF16)
    grad_column[...] = grad_value.T.astype(BF16)
    mask_row = jnp.where(tower_mask, 1.0, 0.0).astype(BF16)
    for g in range(side):
        here = slice(g * quarter, (g + 1) * quarter)
        grad_wide[here] = mm(grad_column[here], mask_row).astype(BF16)

    def tower_back(j, carry):
        group = lax.rem(chip // side + 2 + j, side)
        here = pl.ds(pl.multiple_of(group * quarter, quarter), quarter)

        def one(p, total):
            grad_pre = grad_wide[here] * slope[p, here]
            slope[p, here] = grad_pre
            return total + mm(grad_pre, weights[p, :depth, :], NT)

        def two(p, total):
            return one(2 * p + 1, one(2 * p, total))

        total = lax.fori_loop(0, 4, two, jnp.zeros((quarter, width), F32))
        d_out[pl.ds(group * side, side)] = total.astype(BF16).reshape(side, rows_here, width)

        def send_grads(i, inner):
            to = group * side + i

            @pl.when(to != chip)
            def _():
                remote(
                    d_out.at[to], d_in.at[chip], d_send, d_recv, seg, to * 2 + core, dp
                ).start()

            return inner

        lax.fori_loop(0, side, send_grads, 0)
        return carry

    lax.fori_loop(0, side, tower_back, 0)
    d_in[chip] = d_out[chip]

    def tower_weight_grad(piece):
        main = mm(mixed_turned[...], slope[piece])
        tail = mm(grad_turned[...], hidden[piece])
        tail = jnp.sum(jnp.where(tower_mask, tail, 0.0), axis=0, keepdims=True)
        tail = jnp.where(mask_tower == 0, tail, 0.0)
        return main, tail

    def twin_grads(i, carry):
        k = lax.rem(2 + 3 * i, 4)
        main, tail = tower_weight_grad(k * 2 + 1 - core)
        w_pair_out[k, :depth, :] = main.astype(BF16)
        w_pair_out[k, depth:, :] = tail.astype(BF16)
        remote(
            w_pair_out.at[k], w_pair_in.at[k], tp_send, tp_recv.at[k], seg, twin, dp
        ).start()
        return carry

    lax.fori_loop(0, 4, twin_grads, 0)

    def send_piece(k, to, slot):
        remote(
            w_z_out.at[k], w_z_in.at[slot], tz_send.at[slot], tz_recv.at[slot], *to
        ).start()

    for k in (2, 1, 0, 3):
        main, tail = tower_weight_grad(k * 2 + core)
        wait_bytes(w_pair_in.at[k], tp_recv.at[k])
        main = main + w_pair_in[k, :depth, :].astype(F32)
        tail = tail + w_pair_in[k, depth:, :].astype(F32)
        w_z_out[k, :depth, :] = main.astype(BF16)
        w_z_out[k, depth:, :] = tail.astype(BF16)
        if k == 2:
            send_piece(2, (1 - seg, me, dp), 2)

    wait_bytes(d_in.at[pl.ds(0, chips - 1)], d_recv)
    total = d_in[0].astype(F32)
    for i in range(1, chips):
        total = total + d_in[i].astype(F32)
    b_out[...] = mm(own_table, total.astype(BF16), TN).reshape(count, capacity, width).astype(BF16)

    def spread(i, carry):
        e, z = lax.rem(me + i // 4, count), lax.rem(i, 4)
        to_seg, to_dp = lax.rem(seg + lax.rem(z, 2), 2), lax.rem(dp + z // 2, 2)
        remote(
            b_out.at[e], g_in.at[z_mine * count + me], g_send, g_recv.at[z_mine], to_seg, e, to_dp
        ).start()
        return carry

    lax.fori_loop(1, 4 * count, spread, 0)
    pltpu.make_async_copy(b_out.at[me], g_in.at[z_mine * count + me], g_recv.at[z_mine]).start()

    send_piece(1, (1 - seg, me, dp), 1)
    wait_bytes(w_z_in.at[2], tz_recv.at[2])
    w_z_out[3] = (w_z_out[3].astype(F32) + w_z_in[2].astype(F32)).astype(BF16)
    send_piece(3, (1 - seg, me, 1 - dp), 3)

    def backward(j, carry):
        z = lax.rem(z_mine + j, 4)
        wait_bytes(g_in.at[pl.ds(z * count, count)], g_recv.at[z])
        here = pl.ds(pl.multiple_of(z * slots, slots), slots)
        grads = wide(g_in[pl.ds(z * count, count)])
        g_rows[here] = grads
        grad_active = mm(grads, w_down[...], NT)
        by_gate[here] = (grad_active * by_gate[here].astype(F32)).astype(BF16)
        by_up[here] = (grad_active * by_up[here].astype(F32)).astype(BF16)
        return carry

    lax.fori_loop(0, 4, backward, 0)
    strip = 256

    def gate_grads(j, total):
        cols = pl.ds(pl.multiple_of(j * strip, strip), strip)
        for source, weight, out in ((by_gate, w_gate, out_gate), (by_up, w_up, out_up)):
            grad = mm(x_turned[...], source[:, cols])
            out[:, cols] = grad.astype(BF16)
            term = grad * weight[:, cols].astype(F32)
            for c in range(strip // 128):
                total = total + term[:, c * 128 : (c + 1) * 128]
        return total

    gain_sum = lax.fori_loop(0, hidden_here // strip, gate_grads, jnp.zeros((width, 128), F32))
    gain_row = jnp.sum(gain_sum.T, axis=0, keepdims=True)
    gain_a_out[...] = gain_row / gain[...]
    mine_a = z_mine * 2 + core
    others = []
    for flip_seg in range(2):
        for flip_dp in range(2):
            for flip_core in range(2):
                if flip_seg or flip_dp or flip_core:
                    others.append((flip_seg, flip_dp, flip_core))
    for flip_seg, flip_dp, flip_core in others:
        remote(
            gain_a_out,
            gain_a_in.at[mine_a],
            ga_send,
            ga_recv,
            1 - seg if flip_seg else seg,
            twin if flip_core else me,
            1 - dp if flip_dp else dp,
        ).start()
    gain_a_in[mine_a] = gain_a_out[...]

    def down_grads(j, carry):
        here = pl.ds(pl.multiple_of(j * strip, strip), strip)
        out_down[here] = mm(active_turned[here], g_rows[...]).astype(BF16)
        return carry

    half = hidden_here // strip // 2
    lax.fori_loop(0, half, down_grads, 0)
    wait_bytes(gain_a_in.at[pl.ds(0, 7)], ga_recv)
    part = gain_a_in[0]
    for i in range(1, 8):
        part = part + gain_a_in[i]
    gain_b_out[...] = part

    def send_gain(i, carry):
        to = lax.rem(chip + i, chips)
        remote(gain_b_out, gain_b_in.at[chip], gb_send, gb_recv, seg, to * 2 + core, dp).start()
        return carry

    lax.fori_loop(1, chips, send_gain, 0)
    gain_b_in[chip] = gain_b_out[...]
    lax.fori_loop(half, hidden_here // strip, down_grads, 0)

    tower_sum = w_z_out[0].astype(F32)
    for k in (1, 3):
        wait_bytes(w_z_in.at[k], tz_recv.at[k])
        tower_sum = tower_sum + w_z_in[k].astype(F32)
    for t in range(towers):
        here = slice(t * per_tower, (t + 1) * per_tower)
        out_tower[t] = tower_sum[:width, here].astype(BF16)
        sum_row[t : t + 1, :] = tower_sum[width : width + 1, here]
    out_tower_row[...] = sum_row[0:towers, :].astype(BF16)
    wait_bytes(gain_b_in.at[pl.ds(0, chips - 1)], gb_recv)
    part = gain_b_in[0]
    for i in range(1, chips):
        part = part + gain_b_in[i]
    out_gain[...] = part

    wait_bytes(x_in.at[pl.ds(0, 4 * count - 2)], x_send)
    wait_bytes(aux_in.at[pl.ds(0, chips - 1)], aux_send)
    wait_bytes(r_in.at[pl.ds(0, 4 * count - 1)], p_send)
    wait_bytes(mixed.at[pl.ds(0, chips - 1)], m_send)
    wait_bytes(value_in.at[pl.ds(0, chips - 1)], v_send)
    wait_bytes(d_in.at[pl.ds(0, chips - 1)], d_send)
    wait_bytes(g_in.at[pl.ds(0, 4 * count - 1)], g_send)
    for k in range(1, 4):
        wait_bytes(own_piece, wz_send.at[k])
        wait_bytes(own_piece, tz_send.at[k])
    for k in range(4):
        wait_bytes(own_piece, wp_send.at[k])
    wait_bytes(w_pair_in, tp_send)
    wait_bytes(gain_a_in.at[pl.ds(0, 7)], ga_send)
    wait_bytes(gain_b_in.at[pl.ds(0, chips - 1)], gb_send)


def run_step(loss_scale, count, capacity, *args):
    feats, routes, arms, targets, gain, w_gate, w_up, w_down, tower_in, tower_out = args
    batches, rows_here, width = feats.shape
    hidden_here = w_gate.shape[2]
    cols = 8 * tower_in.shape[2]
    piece = jax.ShapeDtypeStruct((width + 16, cols), BF16)
    chips = count // 2
    blocks = 4 * count
    slots = blocks * capacity
    all_rows = chips * rows_here
    v = pltpu.VMEM
    dma = pltpu.SemaphoreType.DMA
    scratch = [
        v((8, 2 * rows_here), F32),
        v(piece.shape, BF16),
        v((16, cols), F32),
        v((8, tower_in.shape[2]), F32),
        v((all_rows, cols), BF16),
        v((batches, rows_here, count * capacity), BF16),
        v((batches, count, capacity, width), BF16),
        v((blocks, capacity, width), BF16),
        v((width, slots), BF16),
        v((slots, hidden_here), BF16),
        v((slots, hidden_here), BF16),
        v((hidden_here, slots), BF16),
        v((blocks, capacity, width), BF16),
        v((blocks, capacity, width), BF16),
        v((chips, rows_here, width), BF16),
        v((width, all_rows), BF16),
        v((chips, 8, 128), F32),
        v((8,) + piece.shape, BF16),
        v((8, all_rows, cols), BF16),
        v((8, all_rows, cols), BF16),
        v((16, all_rows), F32),
        v((2, all_rows), F32),
        v((chips, 2, all_rows), F32),
        v((16, all_rows), BF16),
        v((all_rows, 16), BF16),
        v((chips, rows_here, width), BF16),
        v((chips, rows_here, width), BF16),
        v((count, capacity, width), BF16),
        v((blocks, capacity, width), BF16),
        v((slots, width), BF16),
        v((4,) + piece.shape, BF16),
        v((4,) + piece.shape, BF16),
        v((4,) + piece.shape, BF16),
        v((4,) + piece.shape, BF16),
        v((1, width), F32),
        v((8, 1, width), F32),
        v((1, width), F32),
        v((chips, 1, width), F32),
        dma(()),
        dma((2,)),
        dma(()),
        dma(()),
        dma(()),
        dma(()),
        dma(()),
        dma((4,)),
        dma(()),
        dma(()),
        dma(()),
        dma(()),
        dma(()),
        dma((4,)),
        dma((4,)),
        dma((4,)),
        dma((4,)),
        dma((4,)),
        dma(()),
        dma((4,)),
        dma((4,)),
        dma((4,)),
        dma(()),
        dma(()),
        dma(()),
        dma(()),
    ]
    out_shape = (
        jax.ShapeDtypeStruct(w_gate.shape, BF16),
        jax.ShapeDtypeStruct(w_up.shape, BF16),
        jax.ShapeDtypeStruct(w_down.shape, BF16),
        jax.ShapeDtypeStruct(tower_in.shape, BF16),
        jax.ShapeDtypeStruct(tower_out.shape, BF16),
        jax.ShapeDtypeStruct((1, width), F32),
    )
    spec = pl.BlockSpec(memory_space=pltpu.VMEM)
    return pl.pallas_call(
        functools.partial(step_kernel, loss_scale),
        out_shape=out_shape,
        in_specs=[spec] * len(args),
        out_specs=(spec,) * len(out_shape),
        scratch_shapes=scratch,
        compiler_params=pltpu.CompilerParams(
            collective_id=0, has_side_effects=True, vmem_limit_bytes=67043328
        ),
    )(*args)


def body(
    features,
    routes,
    arm_ids,
    targets,
    trunk_gain,
    gate_weight,
    up_weight,
    down_weight,
    tower_in,
    tower_out,
):
    batches, rows_here, width = features.shape
    count = lax.axis_size("expert")
    capacity = max(2, 2 * routes.shape[2] * rows_here // count)
    loss_scale = float(batches * rows_here * count * lax.axis_size("dp")) ** (-0.5)
    *grads, grad_gain = run_step(
        loss_scale,
        count,
        capacity,
        features,
        routes,
        arm_ids,
        targets,
        trunk_gain.reshape(1, width),
        gate_weight,
        up_weight,
        down_weight,
        tower_in,
        tower_out,
    )
    return (*grads, grad_gain.reshape(width))


def solution(mesh):
    in_specs = (
        P(None, ("expert", "dp"), None),
        P(None, ("expert", "dp"), None),
        P(None, ("expert", "dp")),
        P(None, ("expert", "dp")),
        P(),
        P("expert", None, ("segment", "dp")),
        P("expert", None, ("segment", "dp")),
        P("expert", ("segment", "dp"), None),
        P(None, None, ("segment", "expert", "dp")),
        P(None, ("segment", "expert", "dp")),
    )
    out_specs = (
        P("expert", None, ("segment", "dp")),
        P("expert", None, ("segment", "dp")),
        P("expert", ("segment", "dp"), None),
        P(None, None, ("segment", "expert", "dp")),
        P(None, ("segment", "expert", "dp")),
        P(),
    )
    return jax.shard_map(body, mesh=mesh, in_specs=in_specs, out_specs=out_specs, check_vma=False)
```

```python
import functools

import jax
import jax.numpy as jnp
from jax import lax
from jax.experimental import pallas as pl
from jax.experimental.pallas import tpu as pltpu
from jax.sharding import PartitionSpec as P

EPSILON = 1e-06
MESH = pl.DeviceIdType.MESH
F32 = jnp.float32
BF16 = jnp.bfloat16
NN = (((1,), (0,)), ((), ()))
NT = (((1,), (1,)), ((), ()))
TN = (((0,), (0,)), ((), ()))


def mm(a, b, dims=NN):
    return lax.dot_general(a, b, dims, preferred_element_type=F32)


def wait_bytes(ref, sem):
    pltpu.make_async_copy(ref, ref, sem).wait()


def sigmoid(value):
    return 0.5 * jnp.tanh(0.5 * value) + 0.5


def wide(block):
    depth, rows, width = block.shape
    return block.astype(F32).reshape(depth * rows, width).astype(BF16)


def step_kernel(
    loss_scale,
    feats,
    routes,
    arms,
    targets,
    gain,
    w_gate,
    w_up,
    w_down,
    tower_in,
    tower_out,
    out_gate,
    out_up,
    out_down,
    out_tower,
    out_tower_row,
    out_gain,
    aux,
    own_piece,
    tail_row,
    sum_row,
    grad_wide,
    tables,
    outgoing,
    x_in,
    x_turned,
    by_gate,
    by_up,
    active_turned,
    p_out,
    r_in,
    mixed,
    mixed_turned,
    aux_in,
    weights,
    hidden,
    slope,
    values,
    value_out,
    value_in,
    grad_turned,
    grad_column,
    d_out,
    d_in,
    b_out,
    g_in,
    g_rows,
    w_pair_out,
    w_pair_in,
    w_z_out,
    w_z_in,
    gain_a_out,
    gain_a_in,
    gain_b_out,
    gain_b_in,
    x_send,
    x_recv,
    aux_send,
    aux_recv,
    p_send,
    p_recv,
    m_send,
    m_recv,
    v_send,
    v_recv,
    d_send,
    d_recv,
    g_send,
    g_recv,
    wz_send,
    wz_recv,
    wp_send,
    wp_recv,
    tp_send,
    tp_recv,
    tz_send,
    tz_recv,
    ga_send,
    ga_recv,
    gb_send,
    gb_recv,
):
    seg, me, dp = lax.axis_index("segment"), lax.axis_index("expert"), lax.axis_index("dp")
    batches, rows_here, width = feats.shape
    count = x_in.shape[0] // 4
    chips = count // 2
    capacity = x_in.shape[1]
    w_gate, w_up, w_down = w_gate.at[0], w_up.at[0], w_down.at[0]
    out_gate, out_up, out_down = out_gate.at[0], out_up.at[0], out_down.at[0]
    hidden_here = w_gate.shape[1]
    towers, per_tower, _ = tower_in.shape
    slots = count * capacity
    chip, core = me // 2, lax.rem(me, 2)
    twin = chip * 2 + 1 - core
    z_mine = dp * 2 + seg
    side = 4
    quarter = rows_here * chips // side
    z_peers = {1: (1 - seg, dp), 2: (seg, 1 - dp), 3: (1 - seg, 1 - dp)}

    def remote(src, dst, send, recv, to_seg, expert, to_dp):
        return pltpu.make_async_remote_copy(
            src_ref=src,
            dst_ref=dst,
            send_sem=send,
            recv_sem=recv,
            device_id=(to_seg, expert, to_dp),
            device_id_type=MESH,
        )

    barrier = pltpu.get_barrier_semaphore()

    def greet(i, carry):
        e, z = i // 4, lax.rem(i, 4)
        pl.semaphore_signal(
            barrier,
            inc=1,
            device_id=(
                lax.rem(seg + lax.rem(z, 2), 2),
                lax.rem(me + e, count),
                lax.rem(dp + z // 2, 2),
            ),
            device_id_type=MESH,
        )
        return carry

    lax.fori_loop(1, 4 * count, greet, 0, unroll=8)

    row_ids = lax.broadcasted_iota(jnp.int32, (rows_here, rows_here), 0)
    col_ids = lax.broadcasted_iota(jnp.int32, (rows_here, rows_here), 1)
    lower = (col_ids < row_ids).astype(F32).astype(BF16)
    expert_ids = lax.broadcasted_iota(jnp.int32, (count, rows_here), 0)
    stretch_row = lax.broadcasted_iota(jnp.int32, (count, slots), 0)
    stretch_col = lax.broadcasted_iota(jnp.int32, (count, slots), 1)
    stretch = (stretch_col // capacity == stretch_row).astype(F32).astype(BF16)
    slot_ids = lax.rem(
        lax.broadcasted_iota(jnp.int32, (rows_here, slots), 1), capacity
    ).astype(F32)
    for b in range(batches):
        wide_rows = feats[b].astype(F32)
        scaled = wide_rows * lax.rsqrt(
            jnp.mean(wide_rows * wide_rows, axis=-1, keepdims=True) + EPSILON
        )
        normed = (scaled * gain[...]).astype(BF16)
        named = routes[b]
        taken = jnp.where(
            (named[0:1, :] == expert_ids) | (named[1:2, :] == expert_ids), 1.0, 0.0
        )
        taken = taken.T.astype(BF16)
        rank = mm(lower, taken).astype(BF16)
        taken_wide = mm(taken, stretch)
        rank_wide = mm(rank, stretch)
        table = jnp.where((taken_wide > 0.5) & (rank_wide == slot_ids), 1.0, 0.0).astype(BF16)
        tables[b] = table
        outgoing[b] = mm(table, normed, TN).reshape(count, capacity, width).astype(BF16)
    pl.semaphore_wait(barrier, 4 * count - 1)

    def dispatch_near(i, carry):
        to = lax.rem(me + i, count)
        for b in range(batches):
            mine = (dp * 2 + b) * count + me
            remote(
                outgoing.at[b, to], x_in.at[mine], x_send, x_recv.at[0], seg, to, dp
            ).start()
        return carry

    def dispatch_far(i, carry):
        to = lax.rem(me + i, count)
        for b in range(batches):
            mine = (dp * 2 + b) * count + me
            remote(
                outgoing.at[b, to], x_in.at[mine], x_send, x_recv.at[1], 1 - seg, to, 1 - dp
            ).start()
        return carry

    lax.fori_loop(1, count, dispatch_near, 0)
    lax.fori_loop(0, count, dispatch_far, 0)
    for b in range(batches):
        pltpu.make_async_copy(
            outgoing.at[b, me], x_in.at[(dp * 2 + b) * count + me], x_recv.at[0]
        ).start()

    def send_weights(k):
        to_seg, to_dp = z_peers[k]
        remote(
            own_piece, weights.at[k * 2 + core], wz_send.at[k], wz_recv.at[k], to_seg, me, to_dp
        ).start()

    def relay_weights(k):
        block = weights.at[k * 2 + core]
        wait_bytes(block, wz_recv.at[k])
        remote(block, block, wp_send.at[k], wp_recv.at[k], seg, twin, dp).start()

    tail_row[...] = jnp.zeros_like(tail_row)
    for t in range(towers):
        tail_row[0:1, t * per_tower : (t + 1) * per_tower] = tower_out[t : t + 1, :].astype(F32)
    blank = jnp.zeros((own_piece.shape[1] - towers * per_tower, width), BF16)
    stacked = jnp.concatenate([tower_in[t] for t in range(towers)] + [blank], axis=0)
    own_piece[:width, :] = stacked.T
    own_piece[width:, :] = tail_row[...].astype(BF16)
    weights[core] = own_piece[...]
    aux[...] = jnp.zeros_like(aux)
    own_targets = jnp.where(seg == 0, targets[0:1, :], targets[1:2, :])
    own_arms = jnp.where(seg == 0, arms[0:1, :], arms[1:2, :]).astype(F32)
    for odd in range(2):

        @pl.when(lax.rem(chip, 2) == odd)
        def _():
            aux[0:1, odd * rows_here : (odd + 1) * rows_here] = own_targets
            aux[1:2, odd * rows_here : (odd + 1) * rows_here] = own_arms

    remote(own_piece, weights.at[core], wp_send.at[0], wp_recv.at[0], seg, twin, dp).start()
    send_weights(1)

    def send_aux(i, carry):
        to = lax.rem(chip + i, chips)
        remote(aux, aux_in.at[chip], aux_send, aux_recv, seg, to * 2 + core, dp).start()
        return carry

    lax.fori_loop(1, chips, send_aux, 0)
    aux_in[chip] = aux[...]

    def forward(j, carry):
        to_dp = lax.rem(dp + j // 2, 2)
        to_seg = lax.rem(j, 2)
        base = (to_dp * 2 + to_seg) * count

        @pl.when(j == 0)
        def _():
            wait_bytes(x_in.at[pl.ds(dp * 2 * count, 2 * count)], x_recv.at[0])

        @pl.when(j == 2)
        def _():
            wait_bytes(x_in.at[pl.ds((1 - dp) * 2 * count, 2 * count)], x_recv.at[1])

        here = pl.ds(pl.multiple_of(base * capacity, slots), slots)
        rows = wide(x_in[pl.ds(base, count)])
        gate_pre = mm(rows, w_gate[...])
        up_pre = mm(rows, w_up[...])
        sig = sigmoid(gate_pre)
        gated = gate_pre * sig
        act = (gated * up_pre).astype(BF16)
        by_up[here] = gated.astype(BF16)
        by_gate[here] = (up_pre * (sig + gated - gated * sig)).astype(BF16)
        half_hidden = hidden_here // 2
        hidden[0, here] = act[:, :half_hidden]
        hidden[1, here] = act[:, half_hidden:]
        made = mm(act, w_down[...])
        p_out[pl.ds(base, count)] = made.reshape(count, capacity, width).astype(BF16)
        local = (to_dp == dp) & (to_seg == seg)

        def give(i, inner):
            e = lax.rem(me + i, count)

            @pl.when((i > 0) | jnp.logical_not(local))
            def _():
                remote(
                    p_out.at[base + e],
                    r_in.at[z_mine * count + me],
                    p_send,
                    p_recv,
                    to_seg,
                    e,
                    to_dp,
                ).start()

            return inner

        lax.fori_loop(0, count, give, 0)

        @pl.when(local)
        def _():
            pltpu.make_async_copy(
                p_out.at[base + me], r_in.at[z_mine * count + me], p_recv
            ).start()

        return carry

    lax.fori_loop(0, 4, forward, 0)
    top = 272
    halves = ((0, pl.ds(0, top)), (3, pl.ds(top, width + 16 - top)))
    for sem, part in halves:
        remote(
            own_piece.at[part],
            weights.at[6 + core, part],
            wz_send.at[sem],
            wz_recv.at[sem],
            1 - seg,
            me,
            1 - dp,
        ).start()

    def relay_half(sem, part):
        block = weights.at[6 + core, part]
        wait_bytes(block, wz_recv.at[sem])
        remote(
            block, weights.at[4 + core, part], wz_send.at[2], wz_recv.at[2], 1 - seg, me, dp
        ).start()

    relay_weights(1)

    def turn(j, carry):
        here = pl.ds(pl.multiple_of(j * slots, slots), slots)
        x_turned[:, here] = wide(x_in[pl.ds(j * count, count)]).T
        active_turned[: hidden_here // 2, here] = hidden[0, here].T
        active_turned[hidden_here // 2 :, here] = hidden[1, here].T
        return carry

    lax.fori_loop(0, 4, turn, 0)

    relay_half(*halves[0])
    wait_bytes(r_in, p_recv)
    own_table = tables[seg]
    added = mm(own_table, wide(r_in[pl.ds(0, count)]))
    for z in range(1, 4):
        added = added + mm(own_table, wide(r_in[pl.ds(z * count, count)]))
    mixed[chip] = (feats[seg].astype(F32) + added).astype(BF16)

    def send_rows(i, carry):
        to = lax.rem(chip + i, chips)
        block = mixed.at[chip]
        remote(block, block, m_send, m_recv.at[chip // side], seg, to * 2 + core, dp).start()
        return carry

    lax.fori_loop(1, chips, send_rows, 0)
    relay_half(*halves[1])
    far = weights.at[6 + core]
    remote(far, far, wp_send.at[3], wp_recv.at[3], seg, twin, dp).start()

    depth = width
    out_cols = own_piece.shape[1]
    mask_tower = lax.broadcasted_iota(jnp.int32, (16, out_cols), 0)
    mask_col = lax.broadcasted_iota(jnp.int32, (16, out_cols), 1) // per_tower
    tower_mask = mask_tower == mask_col

    def out_matrix(piece):
        tail = weights[piece, depth:, :].astype(F32)
        return jnp.where(tower_mask, tail[0:1, :], 0.0).astype(BF16)

    def tower_forward(piece, group, fresh):
        here = pl.ds(pl.multiple_of(group * quarter, quarter), quarter)
        blocks = mixed[pl.ds(group * side, side)]
        rows = blocks.reshape(quarter, width)
        pre_act = mm(rows, weights[piece, :depth, :])
        sig = sigmoid(pre_act)
        hid_wide = pre_act * sig
        hid = hid_wide.astype(BF16)
        hidden[piece, here] = hid
        tail = weights[piece, depth:, :].astype(F32)[0:1, :]
        slope[piece, here] = ((sig + hid_wide - hid_wide * sig) * tail).astype(BF16)
        part = mm(out_matrix(piece), hid, NT)
        if fresh:
            values[:, here] = part
        else:
            values[:, here] += part

    wait_bytes(weights.at[0], wp_recv.at[0])
    for j, ahead in enumerate((0, 1, 3, 2)):
        group = lax.rem(chip // side + ahead, side)
        if ahead == 0:
            wait_bytes(mixed.at[pl.ds(0, side - 1)], m_recv.at[group])
        else:
            wait_bytes(mixed.at[pl.ds(0, side)], m_recv.at[group])
        if j == 0:
            wait_bytes(weights.at[0], wp_recv.at[1])
        tower_forward(0, group, True)

        def more(p, carry, group=group):
            tower_forward(p, group, False)
            return carry

        lax.fori_loop(1, 4, more, 0)
    for k in (3, 2):
        if k == 2:
            relay_weights(2)
        for turn_core in (core, 1 - core):
            if turn_core is not core:
                wait_bytes(weights.at[0], wp_recv.at[k])

            def more_groups(group, carry, piece=k * 2 + turn_core):
                tower_forward(piece, group, False)
                return carry

            lax.fori_loop(0, side, more_groups, 0)

    wait_bytes(aux_in.at[pl.ds(0, chips - 1)], aux_recv)
    pairs = [aux_in[2 * g] + aux_in[2 * g + 1] for g in range(chips // 2)]
    notes = jnp.concatenate(pairs, axis=1)
    all_targets, all_arms = notes[0:1], notes[1:2]
    all_rows = chips * rows_here
    tower_ids = lax.broadcasted_iota(jnp.int32, (16, all_rows), 0).astype(F32)
    arm_mask = tower_ids - 1.0 == all_arms
    every = values[...]
    value_out[0:1] = every[0:1]
    value_out[1:2] = jnp.sum(jnp.where(arm_mask, every, 0.0), axis=0, keepdims=True)

    def send_values(i, carry):
        to = lax.rem(chip + i, chips)
        remote(value_out, value_in.at[chip], v_send, v_recv, seg, to * 2 + core, dp).start()
        return carry

    lax.fori_loop(1, chips, send_values, 0)
    value_in[chip] = value_out[...]
    for g in range(side):
        mixed_turned[:, g * quarter : (g + 1) * quarter] = (
            mixed[g * side : (g + 1) * side].reshape(quarter, width).T
        )
    wait_bytes(value_in.at[pl.ds(0, chips - 1)], v_recv)
    summed = value_in[0]
    for i in range(1, chips):
        summed = summed + value_in[i]
    treated = jnp.where(all_arms != 0.0, 1.0, 0.0)
    grad_first = loss_scale * (sigmoid(summed[0:1]) - treated)
    grad_arm = loss_scale * (summed[1:2] - all_targets)
    grad_value = jnp.where(tower_ids == 0.0, grad_first, jnp.where(arm_mask, grad_arm, 0.0))
    grad_turned[...] = grad_value.astype(BF16)
    grad_column[...] = grad_value.T.astype(BF16)
    mask_row = jnp.where(tower_mask, 1.0, 0.0).astype(BF16)
    for g in range(side):
        here = slice(g * quarter, (g + 1) * quarter)
        grad_wide[here] = mm(grad_column[here], mask_row).astype(BF16)

    def tower_weight_grad(piece):
        main = mm(mixed_turned[...], slope[piece])
        tail = mm(grad_turned[...], hidden[piece])
        tail = jnp.sum(jnp.where(tower_mask, tail, 0.0), axis=0, keepdims=True)
        tail = jnp.where(mask_tower == 0, tail, 0.0)
        return main, tail

    def twin_grads(k):
        main, tail = tower_weight_grad(k * 2 + 1 - core)
        w_pair_out[k, :depth, :] = main.astype(BF16)
        w_pair_out[k, depth:, :] = tail.astype(BF16)
        remote(
            w_pair_out.at[k], w_pair_in.at[k], tp_send, tp_recv.at[k], seg, twin, dp
        ).start()

    def own_grads(k):
        main, tail = tower_weight_grad(k * 2 + core)
        wait_bytes(w_pair_in.at[k], tp_recv.at[k])
        main = main + w_pair_in[k, :depth, :].astype(F32)
        tail = tail + w_pair_in[k, depth:, :].astype(F32)
        w_z_out[k, :depth, :] = main.astype(BF16)
        w_z_out[k, depth:, :] = tail.astype(BF16)

    def send_piece(k, to, slot):
        remote(
            w_z_out.at[k], w_z_in.at[slot], tz_send.at[slot], tz_recv.at[slot], *to
        ).start()

    def slope_to_grad(p, here):
        grad_pre = grad_wide[here] * slope[p, here]
        slope[p, here] = grad_pre
        return grad_pre

    for g in range(side):
        for p in (4, 5):
            slope_to_grad(p, slice(g * quarter, (g + 1) * quarter))

    for j in range(side):
        group = lax.rem(chip // side + (2, 1, 3, 0)[j], side)
        here = pl.ds(pl.multiple_of(group * quarter, quarter), quarter)

        def two(i, total, here=here):
            p = jnp.where(i == 2, 6, 2 * i)
            for q in range(2):
                grad_pre = slope_to_grad(p + q, here)
                total = total + mm(grad_pre, weights[p + q, :depth, :], NT)
            return total

        total = jnp.zeros((quarter, width), F32)
        for p in (4, 5):
            total = total + mm(slope[p, here], weights[p, :depth, :], NT)
        total = lax.fori_loop(0, 3, two, total)
        d_out[pl.ds(group * side, side)] = total.astype(BF16).reshape(side, rows_here, width)

        def send_grads(i, inner, group=group):
            to = group * side + i

            @pl.when(to != chip)
            def _():
                remote(
                    d_out.at[to], d_in.at[chip], d_send, d_recv, seg, to * 2 + core, dp
                ).start()

            return inner

        lax.fori_loop(0, side, send_grads, 0)
        if j == 0:
            twin_grads(2)
        if j == 1:
            own_grads(2)
            send_piece(2, (1 - seg, me, dp), 2)
    d_in[chip] = d_out[chip]
    for k in (1, 3, 0):
        twin_grads(k)
    for k in (1, 3, 0):
        own_grads(k)

    wait_bytes(d_in.at[pl.ds(0, chips - 1)], d_recv)
    total = d_in[0].astype(F32)
    for i in range(1, chips):
        total = total + d_in[i].astype(F32)
    b_out[...] = mm(own_table, total.astype(BF16), TN).reshape(count, capacity, width).astype(BF16)

    def spread(i, carry):
        e, z = lax.rem(me + i // 4, count), lax.rem(i, 4)
        to_seg, to_dp = lax.rem(seg + lax.rem(z, 2), 2), lax.rem(dp + z // 2, 2)
        remote(
            b_out.at[e], g_in.at[z_mine * count + me], g_send, g_recv.at[z_mine], to_seg, e, to_dp
        ).start()
        return carry

    lax.fori_loop(1, 4 * count, spread, 0)
    pltpu.make_async_copy(b_out.at[me], g_in.at[z_mine * count + me], g_recv.at[z_mine]).start()

    send_piece(1, (1 - seg, me, dp), 1)
    wait_bytes(w_z_in.at[2], tz_recv.at[2])
    w_z_out[3] = (w_z_out[3].astype(F32) + w_z_in[2].astype(F32)).astype(BF16)
    send_piece(3, (1 - seg, me, 1 - dp), 3)

    def backward(j, carry):
        z = lax.rem(z_mine + j, 4)
        wait_bytes(g_in.at[pl.ds(z * count, count)], g_recv.at[z])
        here = pl.ds(pl.multiple_of(z * slots, slots), slots)
        grads = wide(g_in[pl.ds(z * count, count)])
        g_rows[here] = grads
        grad_active = mm(grads, w_down[...], NT)
        by_gate[here] = (grad_active * by_gate[here].astype(F32)).astype(BF16)
        by_up[here] = (grad_active * by_up[here].astype(F32)).astype(BF16)
        return carry

    lax.fori_loop(0, 4, backward, 0)
    strip = 256

    def gate_grads(j, total):
        cols = pl.ds(pl.multiple_of(j * strip, strip), strip)
        for source, weight, out in ((by_gate, w_gate, out_gate), (by_up, w_up, out_up)):
            grad = mm(x_turned[...], source[:, cols])
            out[:, cols] = grad.astype(BF16)
            term = grad * weight[:, cols].astype(F32)
            for c in range(strip // 128):
                total = total + term[:, c * 128 : (c + 1) * 128]
        return total

    gain_sum = lax.fori_loop(0, hidden_here // strip, gate_grads, jnp.zeros((width, 128), F32))
    gain_row = jnp.sum(gain_sum.T, axis=0, keepdims=True)
    gain_a_out[...] = gain_row / gain[...]
    mine_a = z_mine * 2 + core
    others = []
    for flip_seg in range(2):
        for flip_dp in range(2):
            for flip_core in range(2):
                if flip_seg or flip_dp or flip_core:
                    others.append((flip_seg, flip_dp, flip_core))
    for flip_seg, flip_dp, flip_core in others:
        remote(
            gain_a_out,
            gain_a_in.at[mine_a],
            ga_send,
            ga_recv,
            1 - seg if flip_seg else seg,
            twin if flip_core else me,
            1 - dp if flip_dp else dp,
        ).start()
    gain_a_in[mine_a] = gain_a_out[...]

    def down_grads(j, carry):
        here = pl.ds(pl.multiple_of(j * strip, strip), strip)
        out_down[here] = mm(active_turned[here], g_rows[...]).astype(BF16)
        return carry

    half = hidden_here // strip // 2
    lax.fori_loop(0, half, down_grads, 0)
    wait_bytes(gain_a_in.at[pl.ds(0, 7)], ga_recv)
    part = gain_a_in[0]
    for i in range(1, 8):
        part = part + gain_a_in[i]
    gain_b_out[...] = part

    def send_gain(i, carry):
        to = lax.rem(chip + i, chips)
        remote(gain_b_out, gain_b_in.at[chip], gb_send, gb_recv, seg, to * 2 + core, dp).start()
        return carry

    lax.fori_loop(1, chips, send_gain, 0)
    gain_b_in[chip] = gain_b_out[...]
    lax.fori_loop(half, hidden_here // strip, down_grads, 0)

    tower_sum = w_z_out[0].astype(F32)
    for k in (1, 3):
        wait_bytes(w_z_in.at[k], tz_recv.at[k])
        tower_sum = tower_sum + w_z_in[k].astype(F32)
    turned_sum = tower_sum[:width].T
    for t in range(towers):
        here = slice(t * per_tower, (t + 1) * per_tower)
        out_tower[t] = turned_sum[here].astype(BF16)
        sum_row[t : t + 1, :] = tower_sum[width : width + 1, here]
    out_tower_row[...] = sum_row[0:towers, :].astype(BF16)
    wait_bytes(gain_b_in.at[pl.ds(0, chips - 1)], gb_recv)
    part = gain_b_in[0]
    for i in range(1, chips):
        part = part + gain_b_in[i]
    out_gain[...] = part

    wait_bytes(x_in.at[pl.ds(0, 4 * count - 2)], x_send)
    wait_bytes(aux_in.at[pl.ds(0, chips - 1)], aux_send)
    wait_bytes(r_in.at[pl.ds(0, 4 * count - 1)], p_send)
    wait_bytes(mixed.at[pl.ds(0, chips - 1)], m_send)
    wait_bytes(value_in.at[pl.ds(0, chips - 1)], v_send)
    wait_bytes(d_in.at[pl.ds(0, chips - 1)], d_send)
    wait_bytes(g_in.at[pl.ds(0, 4 * count - 1)], g_send)
    for k in range(1, 4):
        wait_bytes(own_piece, tz_send.at[k])
    for sem, part in halves:
        wait_bytes(own_piece.at[part], wz_send.at[sem])
    wait_bytes(own_piece, wz_send.at[1])
    wait_bytes(own_piece, wz_send.at[2])
    for k in range(4):
        wait_bytes(own_piece, wp_send.at[k])
    wait_bytes(w_pair_in, tp_send)
    wait_bytes(gain_a_in.at[pl.ds(0, 7)], ga_send)
    wait_bytes(gain_b_in.at[pl.ds(0, chips - 1)], gb_send)


def run_step(loss_scale, count, capacity, *args):
    feats, routes, arms, targets, gain, w_gate, w_up, w_down, tower_in, tower_out = args
    batches, rows_here, width = feats.shape
    hidden_here = w_gate.shape[2]
    cols = 8 * tower_in.shape[1]
    piece = jax.ShapeDtypeStruct((width + 16, cols), BF16)
    chips = count // 2
    blocks = 4 * count
    slots = blocks * capacity
    all_rows = chips * rows_here
    v = pltpu.VMEM
    dma = pltpu.SemaphoreType.DMA
    scratch = [
        v((8, 2 * rows_here), F32),
        v(piece.shape, BF16),
        v((16, cols), F32),
        v((8, tower_in.shape[1]), F32),
        v((all_rows, cols), BF16),
        v((batches, rows_here, count * capacity), BF16),
        v((batches, count, capacity, width), BF16),
        v((blocks, capacity, width), BF16),
        v((width, slots), BF16),
        v((slots, hidden_here), BF16),
        v((slots, hidden_here), BF16),
        v((hidden_here, slots), BF16),
        v((blocks, capacity, width), BF16),
        v((blocks, capacity, width), BF16),
        v((chips, rows_here, width), BF16),
        v((width, all_rows), BF16),
        v((chips, 8, 128), F32),
        v((8,) + piece.shape, BF16),
        v((8, all_rows, cols), BF16),
        v((8, all_rows, cols), BF16),
        v((16, all_rows), F32),
        v((2, all_rows), F32),
        v((chips, 2, all_rows), F32),
        v((16, all_rows), BF16),
        v((all_rows, 16), BF16),
        v((chips, rows_here, width), BF16),
        v((chips, rows_here, width), BF16),
        v((count, capacity, width), BF16),
        v((blocks, capacity, width), BF16),
        v((slots, width), BF16),
        v((4,) + piece.shape, BF16),
        v((4,) + piece.shape, BF16),
        v((4,) + piece.shape, BF16),
        v((4,) + piece.shape, BF16),
        v((1, width), F32),
        v((8, 1, width), F32),
        v((1, width), F32),
        v((chips, 1, width), F32),
        dma(()),
        dma((2,)),
        dma(()),
        dma(()),
        dma(()),
        dma(()),
        dma(()),
        dma((4,)),
        dma(()),
        dma(()),
        dma(()),
        dma(()),
        dma(()),
        dma((4,)),
        dma((4,)),
        dma((4,)),
        dma((4,)),
        dma((4,)),
        dma(()),
        dma((4,)),
        dma((4,)),
        dma((4,)),
        dma(()),
        dma(()),
        dma(()),
        dma(()),
    ]
    out_shape = (
        jax.ShapeDtypeStruct(w_gate.shape, BF16),
        jax.ShapeDtypeStruct(w_up.shape, BF16),
        jax.ShapeDtypeStruct(w_down.shape, BF16),
        jax.ShapeDtypeStruct(tower_in.shape, BF16),
        jax.ShapeDtypeStruct(tower_out.shape, BF16),
        jax.ShapeDtypeStruct((1, width), F32),
    )
    spec = pl.BlockSpec(memory_space=pltpu.VMEM)
    return pl.pallas_call(
        functools.partial(step_kernel, loss_scale),
        out_shape=out_shape,
        in_specs=[spec] * len(args),
        out_specs=(spec,) * len(out_shape),
        scratch_shapes=scratch,
        compiler_params=pltpu.CompilerParams(
            collective_id=0, has_side_effects=True, vmem_limit_bytes=67043328
        ),
    )(*args)


def body(
    features,
    routes,
    arm_ids,
    targets,
    trunk_gain,
    gate_weight,
    up_weight,
    down_weight,
    tower_in,
    tower_out,
):
    batches, rows_here, width = features.shape
    count = lax.axis_size("expert")
    capacity = max(2, 2 * routes.shape[2] * rows_here // count)
    loss_scale = float(batches * rows_here * count * lax.axis_size("dp")) ** (-0.5)
    *grads, grad_gain = run_step(
        loss_scale,
        count,
        capacity,
        features,
        routes.transpose(0, 2, 1),
        arm_ids,
        targets,
        trunk_gain.reshape(1, width),
        gate_weight,
        up_weight,
        down_weight,
        tower_in.transpose(0, 2, 1),
        tower_out,
    )
    grads[3] = grads[3].transpose(0, 2, 1)
    return (*grads, grad_gain.reshape(width))


def solution(mesh):
    in_specs = (
        P(None, ("expert", "dp"), None),
        P(None, ("expert", "dp"), None),
        P(None, ("expert", "dp")),
        P(None, ("expert", "dp")),
        P(),
        P("expert", None, ("segment", "dp")),
        P("expert", None, ("segment", "dp")),
        P("expert", ("segment", "dp"), None),
        P(None, None, ("segment", "expert", "dp")),
        P(None, ("segment", "expert", "dp")),
    )
    out_specs = (
        P("expert", None, ("segment", "dp")),
        P("expert", None, ("segment", "dp")),
        P("expert", ("segment", "dp"), None),
        P(None, None, ("segment", "expert", "dp")),
        P(None, ("segment", "expert", "dp")),
        P(),
    )
    return jax.shard_map(body, mesh=mesh, in_specs=in_specs, out_specs=out_specs, check_vma=False)
```

```python
import functools

import jax
import jax.numpy as jnp
from jax import lax
from jax.experimental import pallas as pl
from jax.experimental.pallas import tpu as pltpu
from jax.sharding import PartitionSpec as P

EPSILON = 1e-06
MESH = pl.DeviceIdType.MESH
F32 = jnp.float32
BF16 = jnp.bfloat16
NN = (((1,), (0,)), ((), ()))
NT = (((1,), (1,)), ((), ()))
TN = (((0,), (0,)), ((), ()))


def mm(a, b, dims=NN):
    return lax.dot_general(a, b, dims, preferred_element_type=F32)


def wait_bytes(ref, sem):
    pltpu.make_async_copy(ref, ref, sem).wait()


def sigmoid(value):
    return 0.5 * jnp.tanh(0.5 * value) + 0.5


def wide(block):
    depth, rows, width = block.shape
    return block.astype(F32).reshape(depth * rows, width).astype(BF16)


def step_kernel(
    loss_scale,
    feats,
    routes,
    arms,
    targets,
    gain,
    w_gate,
    w_up,
    w_down,
    tower_in,
    tower_out,
    out_gate,
    out_up,
    out_down,
    out_tower,
    out_tower_row,
    out_gain,
    aux,
    own_piece,
    tail_row,
    sum_row,
    grad_wide,
    tables,
    outgoing,
    x_in,
    x_turned,
    by_gate,
    by_up,
    active_turned,
    p_out,
    r_in,
    mixed,
    mixed_turned,
    aux_in,
    weights,
    hidden,
    slope,
    values,
    value_out,
    value_in,
    grad_turned,
    grad_column,
    d_out,
    d_in,
    b_out,
    g_in,
    g_rows,
    w_pair_out,
    w_pair_in,
    w_z_out,
    w_z_in,
    gain_a_out,
    gain_a_in,
    gain_b_out,
    gain_b_in,
    x_send,
    x_recv,
    aux_send,
    aux_recv,
    p_send,
    p_recv,
    m_send,
    m_recv,
    v_send,
    v_recv,
    d_send,
    d_recv,
    g_send,
    g_recv,
    wz_send,
    wz_recv,
    wp_send,
    wp_recv,
    tp_send,
    tp_recv,
    tz_send,
    tz_recv,
    ga_send,
    ga_recv,
    gb_send,
    gb_recv,
):
    seg, me, dp = lax.axis_index("segment"), lax.axis_index("expert"), lax.axis_index("dp")
    batches, rows_here, width = feats.shape
    count = x_in.shape[0] // 4
    chips = count // 2
    capacity = x_in.shape[1]
    w_gate, w_up, w_down = w_gate.at[0], w_up.at[0], w_down.at[0]
    out_gate, out_up, out_down = out_gate.at[0], out_up.at[0], out_down.at[0]
    hidden_here = w_gate.shape[1]
    towers, per_tower, _ = tower_in.shape
    slots = count * capacity
    chip, core = me // 2, lax.rem(me, 2)
    twin = chip * 2 + 1 - core
    z_mine = dp * 2 + seg
    side = 4
    quarter = rows_here * chips // side
    z_peers = {1: (1 - seg, dp), 2: (seg, 1 - dp), 3: (1 - seg, 1 - dp)}

    def remote(src, dst, send, recv, to_seg, expert, to_dp):
        return pltpu.make_async_remote_copy(
            src_ref=src,
            dst_ref=dst,
            send_sem=send,
            recv_sem=recv,
            device_id=(to_seg, expert, to_dp),
            device_id_type=MESH,
        )

    barrier = pltpu.get_barrier_semaphore()

    def greet(i, carry):
        e, z = i // 4, lax.rem(i, 4)
        pl.semaphore_signal(
            barrier,
            inc=1,
            device_id=(
                lax.rem(seg + lax.rem(z, 2), 2),
                lax.rem(me + e, count),
                lax.rem(dp + z // 2, 2),
            ),
            device_id_type=MESH,
        )
        return carry

    lax.fori_loop(1, 4 * count, greet, 0, unroll=8)

    row_ids = lax.broadcasted_iota(jnp.int32, (rows_here, rows_here), 0)
    col_ids = lax.broadcasted_iota(jnp.int32, (rows_here, rows_here), 1)
    lower = (col_ids < row_ids).astype(F32).astype(BF16)
    expert_ids = lax.broadcasted_iota(jnp.int32, (count, rows_here), 0)
    stretch_row = lax.broadcasted_iota(jnp.int32, (count, slots), 0)
    stretch_col = lax.broadcasted_iota(jnp.int32, (count, slots), 1)
    stretch = (stretch_col // capacity == stretch_row).astype(F32).astype(BF16)
    slot_ids = lax.rem(
        lax.broadcasted_iota(jnp.int32, (rows_here, slots), 1), capacity
    ).astype(F32)
    for b in range(batches):
        wide_rows = feats[b].astype(F32)
        scaled = wide_rows * lax.rsqrt(
            jnp.mean(wide_rows * wide_rows, axis=-1, keepdims=True) + EPSILON
        )
        normed = (scaled * gain[...]).astype(BF16)
        named = routes[b]
        taken = jnp.where(
            (named[0:1, :] == expert_ids) | (named[1:2, :] == expert_ids), 1.0, 0.0
        )
        taken = taken.T.astype(BF16)
        rank = mm(lower, taken).astype(BF16)
        taken_wide = mm(taken, stretch)
        rank_wide = mm(rank, stretch)
        table = jnp.where((taken_wide > 0.5) & (rank_wide == slot_ids), 1.0, 0.0).astype(BF16)
        tables[b] = table
        outgoing[b] = mm(table, normed, TN).reshape(count, capacity, width).astype(BF16)
    pl.semaphore_wait(barrier, 4 * count - 1)

    def dispatch_near(i, carry):
        to = lax.rem(me + i, count)
        for b in range(batches):
            mine = (dp * 2 + b) * count + me
            remote(
                outgoing.at[b, to], x_in.at[mine], x_send, x_recv.at[0], seg, to, dp
            ).start()
        return carry

    def dispatch_far(i, carry):
        to = lax.rem(me + i, count)
        for b in range(batches):
            mine = (dp * 2 + b) * count + me
            remote(
                outgoing.at[b, to], x_in.at[mine], x_send, x_recv.at[1], 1 - seg, to, 1 - dp
            ).start()
        return carry

    lax.fori_loop(1, count, dispatch_near, 0)
    lax.fori_loop(0, count, dispatch_far, 0)
    for b in range(batches):
        pltpu.make_async_copy(
            outgoing.at[b, me], x_in.at[(dp * 2 + b) * count + me], x_recv.at[0]
        ).start()

    def send_weights(k):
        to_seg, to_dp = z_peers[k]
        remote(
            own_piece, weights.at[k * 2 + core], wz_send.at[k], wz_recv.at[k], to_seg, me, to_dp
        ).start()

    def relay_weights(k):
        block = weights.at[k * 2 + core]
        wait_bytes(block, wz_recv.at[k])
        remote(block, block, wp_send.at[k], wp_recv.at[k], seg, twin, dp).start()

    tail_row[...] = jnp.zeros_like(tail_row)
    for t in range(towers):
        tail_row[0:1, t * per_tower : (t + 1) * per_tower] = tower_out[t : t + 1, :].astype(F32)
    blank = jnp.zeros((own_piece.shape[1] - towers * per_tower, width), BF16)
    stacked = jnp.concatenate([tower_in[t] for t in range(towers)] + [blank], axis=0)
    own_piece[:width, :] = stacked.T
    own_piece[width:, :] = tail_row[...].astype(BF16)
    weights[core] = own_piece[...]
    aux[...] = jnp.zeros_like(aux)
    own_targets = jnp.where(seg == 0, targets[0:1, :], targets[1:2, :])
    own_arms = jnp.where(seg == 0, arms[0:1, :], arms[1:2, :]).astype(F32)
    for odd in range(2):

        @pl.when(lax.rem(chip, 2) == odd)
        def _():
            aux[0:1, odd * rows_here : (odd + 1) * rows_here] = own_targets
            aux[1:2, odd * rows_here : (odd + 1) * rows_here] = own_arms

    remote(own_piece, weights.at[core], wp_send.at[0], wp_recv.at[0], seg, twin, dp).start()
    send_weights(1)

    def send_aux(i, carry):
        to = lax.rem(chip + i, chips)
        remote(aux, aux_in.at[chip], aux_send, aux_recv, seg, to * 2 + core, dp).start()
        return carry

    lax.fori_loop(1, chips, send_aux, 0)
    aux_in[chip] = aux[...]

    def forward(j, carry):
        to_dp = lax.rem(dp + j // 2, 2)
        to_seg = lax.rem(j, 2)
        base = (to_dp * 2 + to_seg) * count

        @pl.when(j == 0)
        def _():
            wait_bytes(x_in.at[pl.ds(dp * 2 * count, 2 * count)], x_recv.at[0])

        @pl.when(j == 2)
        def _():
            wait_bytes(x_in.at[pl.ds((1 - dp) * 2 * count, 2 * count)], x_recv.at[1])

        here = pl.ds(pl.multiple_of(base * capacity, slots), slots)
        rows = wide(x_in[pl.ds(base, count)])
        gate_pre = mm(rows, w_gate[...])
        up_pre = mm(rows, w_up[...])
        sig = sigmoid(gate_pre)
        gated = gate_pre * sig
        act = (gated * up_pre).astype(BF16)
        by_up[here] = gated.astype(BF16)
        by_gate[here] = (up_pre * (sig + gated - gated * sig)).astype(BF16)
        half_hidden = hidden_here // 2
        hidden[0, here] = act[:, :half_hidden]
        hidden[1, here] = act[:, half_hidden:]
        made = mm(act, w_down[...])
        p_out[pl.ds(base, count)] = made.reshape(count, capacity, width).astype(BF16)
        local = (to_dp == dp) & (to_seg == seg)

        def give(i, inner):
            e = lax.rem(me + i, count)

            @pl.when((i > 0) | jnp.logical_not(local))
            def _():
                remote(
                    p_out.at[base + e],
                    r_in.at[z_mine * count + me],
                    p_send,
                    p_recv,
                    to_seg,
                    e,
                    to_dp,
                ).start()

            return inner

        lax.fori_loop(0, count, give, 0)

        @pl.when(local)
        def _():
            pltpu.make_async_copy(
                p_out.at[base + me], r_in.at[z_mine * count + me], p_recv
            ).start()

        return carry

    lax.fori_loop(0, 4, forward, 0)
    top = 272
    halves = ((0, pl.ds(0, top)), (3, pl.ds(top, width + 16 - top)))
    for sem, part in halves:
        remote(
            own_piece.at[part],
            weights.at[6 + core, part],
            wz_send.at[sem],
            wz_recv.at[sem],
            1 - seg,
            me,
            1 - dp,
        ).start()

    def relay_half(sem, part):
        block = weights.at[6 + core, part]
        wait_bytes(block, wz_recv.at[sem])
        remote(
            block, weights.at[4 + core, part], wz_send.at[2], wz_recv.at[2], 1 - seg, me, dp
        ).start()

    relay_weights(1)

    def turn(j, carry):
        here = pl.ds(pl.multiple_of(j * slots, slots), slots)
        x_turned[:, here] = wide(x_in[pl.ds(j * count, count)]).T
        active_turned[: hidden_here // 2, here] = hidden[0, here].T
        active_turned[hidden_here // 2 :, here] = hidden[1, here].T
        return carry

    lax.fori_loop(0, 4, turn, 0)

    wait_bytes(r_in, p_recv)
    own_table = tables[seg]
    added = mm(own_table, wide(r_in[pl.ds(0, count)]))
    for z in range(1, 4):
        added = added + mm(own_table, wide(r_in[pl.ds(z * count, count)]))
    mixed[chip] = (feats[seg].astype(F32) + added).astype(BF16)

    across, along = chip // side, lax.rem(chip, side)
    for ahead in (0, 1, 3, 2):

        def send_rows(i, carry, ahead=ahead):
            to = lax.rem(across + ahead, side) * side + lax.rem(along + i, side)
            block = mixed.at[chip]
            remote(block, block, m_send, m_recv.at[across], seg, to * 2 + core, dp).start()
            return carry

        lax.fori_loop(0 if ahead else 1, side, send_rows, 0)

    depth = width
    out_cols = own_piece.shape[1]
    mask_tower = lax.broadcasted_iota(jnp.int32, (16, out_cols), 0)
    mask_col = lax.broadcasted_iota(jnp.int32, (16, out_cols), 1) // per_tower
    tower_mask = mask_tower == mask_col

    def out_matrix(piece):
        tail = weights[piece, depth:, :].astype(F32)
        return jnp.where(tower_mask, tail[0:1, :], 0.0).astype(BF16)

    def tower_forward(piece, group, fresh):
        here = pl.ds(pl.multiple_of(group * quarter, quarter), quarter)
        blocks = mixed[pl.ds(group * side, side)]
        rows = blocks.reshape(quarter, width)
        pre_act = mm(rows, weights[piece, :depth, :])
        sig = sigmoid(pre_act)
        hid_wide = pre_act * sig
        hid = hid_wide.astype(BF16)
        hidden[piece, here] = hid
        tail = weights[piece, depth:, :].astype(F32)[0:1, :]
        slope[piece, here] = ((sig + hid_wide - hid_wide * sig) * tail).astype(BF16)
        part = mm(out_matrix(piece), hid, NT)
        if fresh:
            values[:, here] = part
        else:
            values[:, here] += part

    wait_bytes(weights.at[0], wp_recv.at[0])
    for j, ahead in enumerate((0, 3, 1, 2)):
        group = lax.rem(across + ahead, side)
        if ahead == 0:
            wait_bytes(mixed.at[pl.ds(0, side - 1)], m_recv.at[group])
        else:
            wait_bytes(mixed.at[pl.ds(0, side)], m_recv.at[group])
        if j == 0:
            wait_bytes(weights.at[0], wp_recv.at[1])
        tower_forward(0, group, True)

        def more(p, carry, group=group):
            tower_forward(p, group, False)
            return carry

        lax.fori_loop(1, 4, more, 0)
        if j == 0:
            relay_half(*halves[0])
        if j == 1:
            relay_half(*halves[1])
            far = weights.at[6 + core]
            remote(far, far, wp_send.at[3], wp_recv.at[3], seg, twin, dp).start()
    for k in (3, 2):
        if k == 2:
            relay_weights(2)
        for turn_core in (core, 1 - core):
            if turn_core is not core:
                wait_bytes(weights.at[0], wp_recv.at[k])

            def more_groups(group, carry, piece=k * 2 + turn_core):
                tower_forward(piece, group, False)
                return carry

            lax.fori_loop(0, side, more_groups, 0)

    wait_bytes(aux_in.at[pl.ds(0, chips - 1)], aux_recv)
    pairs = [aux_in[2 * g] + aux_in[2 * g + 1] for g in range(chips // 2)]
    notes = jnp.concatenate(pairs, axis=1)
    all_targets, all_arms = notes[0:1], notes[1:2]
    all_rows = chips * rows_here
    tower_ids = lax.broadcasted_iota(jnp.int32, (16, all_rows), 0).astype(F32)
    arm_mask = tower_ids - 1.0 == all_arms
    every = values[...]
    value_out[0:1] = every[0:1]
    value_out[1:2] = jnp.sum(jnp.where(arm_mask, every, 0.0), axis=0, keepdims=True)

    def send_values(i, carry):
        to = lax.rem(chip + i, chips)
        remote(value_out, value_in.at[chip], v_send, v_recv, seg, to * 2 + core, dp).start()
        return carry

    lax.fori_loop(1, chips, send_values, 0)
    value_in[chip] = value_out[...]
    for g in range(side):
        mixed_turned[:, g * quarter : (g + 1) * quarter] = (
            mixed[g * side : (g + 1) * side].reshape(quarter, width).T
        )
    wait_bytes(value_in.at[pl.ds(0, chips - 1)], v_recv)
    summed = value_in[0]
    for i in range(1, chips):
        summed = summed + value_in[i]
    treated = jnp.where(all_arms != 0.0, 1.0, 0.0)
    grad_first = loss_scale * (sigmoid(summed[0:1]) - treated)
    grad_arm = loss_scale * (summed[1:2] - all_targets)
    grad_value = jnp.where(tower_ids == 0.0, grad_first, jnp.where(arm_mask, grad_arm, 0.0))
    grad_turned[...] = grad_value.astype(BF16)
    grad_column[...] = grad_value.T.astype(BF16)
    mask_row = jnp.where(tower_mask, 1.0, 0.0).astype(BF16)
    for g in range(side):
        here = slice(g * quarter, (g + 1) * quarter)
        grad_wide[here] = mm(grad_column[here], mask_row).astype(BF16)

    def tower_weight_grad(piece):
        main = mm(mixed_turned[...], slope[piece])
        tail = mm(grad_turned[...], hidden[piece])
        tail = jnp.sum(jnp.where(tower_mask, tail, 0.0), axis=0, keepdims=True)
        tail = jnp.where(mask_tower == 0, tail, 0.0)
        return main, tail

    def twin_grads(k):
        main, tail = tower_weight_grad(k * 2 + 1 - core)
        w_pair_out[k, :depth, :] = main.astype(BF16)
        w_pair_out[k, depth:, :] = tail.astype(BF16)
        remote(
            w_pair_out.at[k], w_pair_in.at[k], tp_send, tp_recv.at[k], seg, twin, dp
        ).start()

    def own_grads(k):
        main, tail = tower_weight_grad(k * 2 + core)
        wait_bytes(w_pair_in.at[k], tp_recv.at[k])
        main = main + w_pair_in[k, :depth, :].astype(F32)
        tail = tail + w_pair_in[k, depth:, :].astype(F32)
        w_z_out[k, :depth, :] = main.astype(BF16)
        w_z_out[k, depth:, :] = tail.astype(BF16)

    inner, outer = (1 - seg, me, dp), (1 - seg, me, 1 - dp)
    upper, lower_part = halves[0][1], halves[1][1]

    def send_piece(k, part, to, sem):
        remote(
            w_z_out.at[k, part], w_z_in.at[k, part], tz_send.at[sem], tz_recv.at[sem], *to
        ).start()

    def add_passing(k, part, sem):
        passing = w_z_in.at[2, part]
        wait_bytes(passing, tz_recv.at[sem])
        w_z_out[k, part] = (w_z_out[k, part].astype(F32) + passing[...].astype(F32)).astype(BF16)

    def slope_to_grad(p, here):
        grad_pre = grad_wide[here] * slope[p, here]
        slope[p, here] = grad_pre
        return grad_pre

    for g in range(side):
        for p in (4, 5):
            slope_to_grad(p, slice(g * quarter, (g + 1) * quarter))

    for j in range(side):
        group = lax.rem(chip // side + (2, 1, 3, 0)[j], side)
        here = pl.ds(pl.multiple_of(group * quarter, quarter), quarter)

        def two(i, total, here=here):
            p = jnp.where(i == 2, 6, 2 * i)
            for q in range(2):
                grad_pre = slope_to_grad(p + q, here)
                total = total + mm(grad_pre, weights[p + q, :depth, :], NT)
            return total

        total = jnp.zeros((quarter, width), F32)
        for p in (4, 5):
            total = total + mm(slope[p, here], weights[p, :depth, :], NT)
        total = lax.fori_loop(0, 3, two, total)
        d_out[pl.ds(group * side, side)] = total.astype(BF16).reshape(side, rows_here, width)

        def send_grads(i, inner, group=group):
            to = group * side + i

            @pl.when(to != chip)
            def _():
                remote(
                    d_out.at[to], d_in.at[chip], d_send, d_recv, seg, to * 2 + core, dp
                ).start()

            return inner

        lax.fori_loop(0, side, send_grads, 0)
        if j == 0:
            twin_grads(2)
        if j == 1:
            own_grads(2)
            send_piece(2, upper, inner, 0)
            send_piece(2, lower_part, outer, 1)
    d_in[chip] = d_out[chip]
    twin_grads(1)
    twin_grads(3)
    own_grads(1)
    send_piece(1, upper, inner, 2)
    own_grads(3)
    send_piece(3, lower_part, outer, 5)
    twin_grads(0)
    own_grads(0)

    wait_bytes(d_in.at[pl.ds(0, chips - 1)], d_recv)
    total = d_in[0].astype(F32)
    for i in range(1, chips):
        total = total + d_in[i].astype(F32)
    b_out[...] = mm(own_table, total.astype(BF16), TN).reshape(count, capacity, width).astype(BF16)

    def spread(i, carry):
        e, z = lax.rem(me + i // 4, count), lax.rem(i, 4)
        to_seg, to_dp = lax.rem(seg + lax.rem(z, 2), 2), lax.rem(dp + z // 2, 2)
        remote(
            b_out.at[e], g_in.at[z_mine * count + me], g_send, g_recv.at[z_mine], to_seg, e, to_dp
        ).start()
        return carry

    lax.fori_loop(1, 4 * count, spread, 0)
    pltpu.make_async_copy(b_out.at[me], g_in.at[z_mine * count + me], g_recv.at[z_mine]).start()

    add_passing(3, upper, 0)
    send_piece(3, upper, outer, 4)
    add_passing(1, lower_part, 1)
    send_piece(1, lower_part, inner, 3)

    def backward(j, carry):
        z = lax.rem(z_mine + j, 4)
        wait_bytes(g_in.at[pl.ds(z * count, count)], g_recv.at[z])
        here = pl.ds(pl.multiple_of(z * slots, slots), slots)
        grads = wide(g_in[pl.ds(z * count, count)])
        g_rows[here] = grads
        grad_active = mm(grads, w_down[...], NT)
        by_gate[here] = (grad_active * by_gate[here].astype(F32)).astype(BF16)
        by_up[here] = (grad_active * by_up[here].astype(F32)).astype(BF16)
        return carry

    lax.fori_loop(0, 4, backward, 0)
    strip = 256

    def gate_grads(j, total):
        cols = pl.ds(pl.multiple_of(j * strip, strip), strip)
        for source, weight, out in ((by_gate, w_gate, out_gate), (by_up, w_up, out_up)):
            grad = mm(x_turned[...], source[:, cols])
            out[:, cols] = grad.astype(BF16)
            term = grad * weight[:, cols].astype(F32)
            for c in range(strip // 128):
                total = total + term[:, c * 128 : (c + 1) * 128]
        return total

    gain_sum = lax.fori_loop(0, hidden_here // strip, gate_grads, jnp.zeros((width, 128), F32))
    gain_row = jnp.sum(gain_sum.T, axis=0, keepdims=True)
    gain_a_out[...] = gain_row / gain[...]
    mine_a = z_mine * 2 + core
    others = []
    for flip_seg in range(2):
        for flip_dp in range(2):
            for flip_core in range(2):
                if flip_seg or flip_dp or flip_core:
                    others.append((flip_seg, flip_dp, flip_core))
    for flip_seg, flip_dp, flip_core in others:
        remote(
            gain_a_out,
            gain_a_in.at[mine_a],
            ga_send,
            ga_recv,
            1 - seg if flip_seg else seg,
            twin if flip_core else me,
            1 - dp if flip_dp else dp,
        ).start()
    gain_a_in[mine_a] = gain_a_out[...]

    def down_grads(j, carry):
        here = pl.ds(pl.multiple_of(j * strip, strip), strip)
        out_down[here] = mm(active_turned[here], g_rows[...]).astype(BF16)
        return carry

    half = hidden_here // strip // 2
    lax.fori_loop(0, half, down_grads, 0)
    wait_bytes(gain_a_in.at[pl.ds(0, 7)], ga_recv)
    part = gain_a_in[0]
    for i in range(1, 8):
        part = part + gain_a_in[i]
    gain_b_out[...] = part

    def send_gain(i, carry):
        to = lax.rem(chip + i, chips)
        remote(gain_b_out, gain_b_in.at[chip], gb_send, gb_recv, seg, to * 2 + core, dp).start()
        return carry

    lax.fori_loop(1, chips, send_gain, 0)
    gain_b_in[chip] = gain_b_out[...]
    lax.fori_loop(half, hidden_here // strip, down_grads, 0)

    tower_sum = w_z_out[0].astype(F32)
    for k, part, sem in (
        (1, upper, 2),
        (1, lower_part, 3),
        (3, upper, 4),
        (3, lower_part, 5),
    ):
        wait_bytes(w_z_in.at[k, part], tz_recv.at[sem])
    for k in (1, 3):
        tower_sum = tower_sum + w_z_in[k].astype(F32)
    turned_sum = tower_sum[:width].T
    for t in range(towers):
        here = slice(t * per_tower, (t + 1) * per_tower)
        out_tower[t] = turned_sum[here].astype(BF16)
        sum_row[t : t + 1, :] = tower_sum[width : width + 1, here]
    out_tower_row[...] = sum_row[0:towers, :].astype(BF16)
    wait_bytes(gain_b_in.at[pl.ds(0, chips - 1)], gb_recv)
    part = gain_b_in[0]
    for i in range(1, chips):
        part = part + gain_b_in[i]
    out_gain[...] = part

    wait_bytes(x_in.at[pl.ds(0, 4 * count - 2)], x_send)
    wait_bytes(aux_in.at[pl.ds(0, chips - 1)], aux_send)
    wait_bytes(r_in.at[pl.ds(0, 4 * count - 1)], p_send)
    wait_bytes(mixed.at[pl.ds(0, chips - 1)], m_send)
    wait_bytes(value_in.at[pl.ds(0, chips - 1)], v_send)
    wait_bytes(d_in.at[pl.ds(0, chips - 1)], d_send)
    wait_bytes(g_in.at[pl.ds(0, 4 * count - 1)], g_send)
    for sem, part in enumerate((upper, lower_part, upper, lower_part, upper, lower_part)):
        wait_bytes(own_piece.at[part], tz_send.at[sem])
    for sem, part in halves:
        wait_bytes(own_piece.at[part], wz_send.at[sem])
    wait_bytes(own_piece, wz_send.at[1])
    wait_bytes(own_piece, wz_send.at[2])
    for k in range(4):
        wait_bytes(own_piece, wp_send.at[k])
    wait_bytes(w_pair_in, tp_send)
    wait_bytes(gain_a_in.at[pl.ds(0, 7)], ga_send)
    wait_bytes(gain_b_in.at[pl.ds(0, chips - 1)], gb_send)


def run_step(loss_scale, count, capacity, *args):
    feats, routes, arms, targets, gain, w_gate, w_up, w_down, tower_in, tower_out = args
    batches, rows_here, width = feats.shape
    hidden_here = w_gate.shape[2]
    cols = 8 * tower_in.shape[1]
    piece = jax.ShapeDtypeStruct((width + 16, cols), BF16)
    chips = count // 2
    blocks = 4 * count
    slots = blocks * capacity
    all_rows = chips * rows_here
    v = pltpu.VMEM
    dma = pltpu.SemaphoreType.DMA
    scratch = [
        v((8, 2 * rows_here), F32),
        v(piece.shape, BF16),
        v((16, cols), F32),
        v((8, tower_in.shape[1]), F32),
        v((all_rows, cols), BF16),
        v((batches, rows_here, count * capacity), BF16),
        v((batches, count, capacity, width), BF16),
        v((blocks, capacity, width), BF16),
        v((width, slots), BF16),
        v((slots, hidden_here), BF16),
        v((slots, hidden_here), BF16),
        v((hidden_here, slots), BF16),
        v((blocks, capacity, width), BF16),
        v((blocks, capacity, width), BF16),
        v((chips, rows_here, width), BF16),
        v((width, all_rows), BF16),
        v((chips, 8, 128), F32),
        v((8,) + piece.shape, BF16),
        v((8, all_rows, cols), BF16),
        v((8, all_rows, cols), BF16),
        v((16, all_rows), F32),
        v((2, all_rows), F32),
        v((chips, 2, all_rows), F32),
        v((16, all_rows), BF16),
        v((all_rows, 16), BF16),
        v((chips, rows_here, width), BF16),
        v((chips, rows_here, width), BF16),
        v((count, capacity, width), BF16),
        v((blocks, capacity, width), BF16),
        v((slots, width), BF16),
        v((4,) + piece.shape, BF16),
        v((4,) + piece.shape, BF16),
        v((4,) + piece.shape, BF16),
        v((4,) + piece.shape, BF16),
        v((1, width), F32),
        v((8, 1, width), F32),
        v((1, width), F32),
        v((chips, 1, width), F32),
        dma(()),
        dma((2,)),
        dma(()),
        dma(()),
        dma(()),
        dma(()),
        dma(()),
        dma((4,)),
        dma(()),
        dma(()),
        dma(()),
        dma(()),
        dma(()),
        dma((4,)),
        dma((4,)),
        dma((4,)),
        dma((4,)),
        dma((4,)),
        dma(()),
        dma((4,)),
        dma((6,)),
        dma((6,)),
        dma(()),
        dma(()),
        dma(()),
        dma(()),
    ]
    out_shape = (
        jax.ShapeDtypeStruct(w_gate.shape, BF16),
        jax.ShapeDtypeStruct(w_up.shape, BF16),
        jax.ShapeDtypeStruct(w_down.shape, BF16),
        jax.ShapeDtypeStruct(tower_in.shape, BF16),
        jax.ShapeDtypeStruct(tower_out.shape, BF16),
        jax.ShapeDtypeStruct((1, width), F32),
    )
    spec = pl.BlockSpec(memory_space=pltpu.VMEM)
    return pl.pallas_call(
        functools.partial(step_kernel, loss_scale),
        out_shape=out_shape,
        in_specs=[spec] * len(args),
        out_specs=(spec,) * len(out_shape),
        scratch_shapes=scratch,
        compiler_params=pltpu.CompilerParams(
            collective_id=0, has_side_effects=True, vmem_limit_bytes=67043328
        ),
    )(*args)


def body(
    features,
    routes,
    arm_ids,
    targets,
    trunk_gain,
    gate_weight,
    up_weight,
    down_weight,
    tower_in,
    tower_out,
):
    batches, rows_here, width = features.shape
    count = lax.axis_size("expert")
    capacity = max(2, 2 * routes.shape[2] * rows_here // count)
    loss_scale = float(batches * rows_here * count * lax.axis_size("dp")) ** (-0.5)
    *grads, grad_gain = run_step(
        loss_scale,
        count,
        capacity,
        features,
        routes.transpose(0, 2, 1),
        arm_ids,
        targets,
        trunk_gain.reshape(1, width),
        gate_weight,
        up_weight,
        down_weight,
        tower_in.transpose(0, 2, 1),
        tower_out,
    )
    grads[3] = grads[3].transpose(0, 2, 1)
    return (*grads, grad_gain.reshape(width))


def solution(mesh):
    in_specs = (
        P(None, ("expert", "dp"), None),
        P(None, ("expert", "dp"), None),
        P(None, ("expert", "dp")),
        P(None, ("expert", "dp")),
        P(),
        P("expert", None, ("segment", "dp")),
        P("expert", None, ("segment", "dp")),
        P("expert", ("segment", "dp"), None),
        P(None, None, ("segment", "expert", "dp")),
        P(None, ("segment", "expert", "dp")),
    )
    out_specs = (
        P("expert", None, ("segment", "dp")),
        P("expert", None, ("segment", "dp")),
        P("expert", ("segment", "dp"), None),
        P(None, None, ("segment", "expert", "dp")),
        P(None, ("segment", "expert", "dp")),
        P(),
    )
    return jax.shard_map(body, mesh=mesh, in_specs=in_specs, out_specs=out_specs, check_vma=False)
```

```python
import functools

import jax
import jax.numpy as jnp
from jax import lax
from jax.experimental import pallas as pl
from jax.experimental.pallas import tpu as pltpu
from jax.sharding import PartitionSpec as P

EPSILON = 1e-06
MESH = pl.DeviceIdType.MESH
F32 = jnp.float32
BF16 = jnp.bfloat16
NN = (((1,), (0,)), ((), ()))
NT = (((1,), (1,)), ((), ()))
TN = (((0,), (0,)), ((), ()))


def mm(a, b, dims=NN):
    return lax.dot_general(a, b, dims, preferred_element_type=F32)


def wait_bytes(ref, sem):
    pltpu.make_async_copy(ref, ref, sem).wait()


def sigmoid(value):
    return 0.5 * jnp.tanh(0.5 * value) + 0.5


def wide(block):
    depth, rows, width = block.shape
    return block.astype(F32).reshape(depth * rows, width).astype(BF16)


def step_kernel(
    loss_scale,
    feats,
    routes,
    arms,
    targets,
    gain,
    w_gate,
    w_up,
    w_down,
    tower_in,
    tower_out,
    out_gate,
    out_up,
    out_down,
    out_tower,
    out_tower_row,
    out_gain,
    aux,
    own_piece,
    tail_row,
    sum_row,
    grad_wide,
    tables,
    outgoing,
    x_in,
    x_turned,
    by_gate,
    by_up,
    active_turned,
    p_out,
    r_in,
    mixed,
    mixed_turned,
    aux_in,
    weights,
    hidden,
    slope,
    values,
    value_out,
    value_in,
    grad_turned,
    grad_column,
    d_out,
    d_in,
    b_out,
    g_in,
    g_rows,
    w_pair_out,
    w_pair_in,
    w_z_out,
    w_z_in,
    gain_a_out,
    gain_a_in,
    gain_b_out,
    gain_b_in,
    x_send,
    x_recv,
    aux_send,
    aux_recv,
    p_send,
    p_recv,
    m_send,
    m_recv,
    v_send,
    v_recv,
    d_send,
    d_recv,
    g_send,
    g_recv,
    wz_send,
    wz_recv,
    wp_send,
    wp_recv,
    tp_send,
    tp_recv,
    tz_send,
    tz_recv,
    ga_send,
    ga_recv,
    gb_send,
    gb_recv,
):
    seg, me, dp = lax.axis_index("segment"), lax.axis_index("expert"), lax.axis_index("dp")
    batches, rows_here, width = feats.shape
    count = x_in.shape[0] // 4
    chips = count // 2
    capacity = x_in.shape[1]
    w_gate, w_up, w_down = w_gate.at[0], w_up.at[0], w_down.at[0]
    out_gate, out_up, out_down = out_gate.at[0], out_up.at[0], out_down.at[0]
    hidden_here = w_gate.shape[1]
    towers, per_tower, _ = tower_in.shape
    slots = count * capacity
    chip, core = me // 2, lax.rem(me, 2)
    twin = chip * 2 + 1 - core
    z_mine = dp * 2 + seg
    side = 4
    quarter = rows_here * chips // side
    z_peers = {1: (1 - seg, dp), 2: (seg, 1 - dp), 3: (1 - seg, 1 - dp)}

    def remote(src, dst, send, recv, to_seg, expert, to_dp):
        return pltpu.make_async_remote_copy(
            src_ref=src,
            dst_ref=dst,
            send_sem=send,
            recv_sem=recv,
            device_id=(to_seg, expert, to_dp),
            device_id_type=MESH,
        )

    barrier = pltpu.get_barrier_semaphore()

    def greet(i, carry):
        e, z = i // 4, lax.rem(i, 4)
        pl.semaphore_signal(
            barrier,
            inc=1,
            device_id=(
                lax.rem(seg + lax.rem(z, 2), 2),
                lax.rem(me + e, count),
                lax.rem(dp + z // 2, 2),
            ),
            device_id_type=MESH,
        )
        return carry

    lax.fori_loop(1, 4 * count, greet, 0, unroll=8)

    row_ids = lax.broadcasted_iota(jnp.int32, (rows_here, rows_here), 0)
    col_ids = lax.broadcasted_iota(jnp.int32, (rows_here, rows_here), 1)
    lower = (col_ids < row_ids).astype(F32).astype(BF16)
    expert_ids = lax.broadcasted_iota(jnp.int32, (count, rows_here), 0)
    stretch_row = lax.broadcasted_iota(jnp.int32, (count, slots), 0)
    stretch_col = lax.broadcasted_iota(jnp.int32, (count, slots), 1)
    stretch = (stretch_col // capacity == stretch_row).astype(F32).astype(BF16)
    slot_ids = lax.rem(
        lax.broadcasted_iota(jnp.int32, (rows_here, slots), 1), capacity
    ).astype(F32)
    for b in range(batches):
        wide_rows = feats[b].astype(F32)
        scaled = wide_rows * lax.rsqrt(
            jnp.mean(wide_rows * wide_rows, axis=-1, keepdims=True) + EPSILON
        )
        normed = (scaled * gain[...]).astype(BF16)
        named = routes[b]
        taken = jnp.where(
            (named[0:1, :] == expert_ids) | (named[1:2, :] == expert_ids), 1.0, 0.0
        )
        taken = taken.T.astype(BF16)
        rank = mm(lower, taken).astype(BF16)
        taken_wide = mm(taken, stretch)
        rank_wide = mm(rank, stretch)
        table = jnp.where((taken_wide > 0.5) & (rank_wide == slot_ids), 1.0, 0.0).astype(BF16)
        tables[b] = table
        outgoing[b] = mm(table, normed, TN).reshape(count, capacity, width).astype(BF16)
    pl.semaphore_wait(barrier, 4 * count - 1)

    def dispatch_near(i, carry):
        to = lax.rem(me + i, count)
        for b in range(batches):
            mine = (dp * 2 + b) * count + me
            remote(
                outgoing.at[b, to], x_in.at[mine], x_send, x_recv.at[0], seg, to, dp
            ).start()
        return carry

    def dispatch_far(i, carry):
        to = lax.rem(me + i, count)
        for b in range(batches):
            mine = (dp * 2 + b) * count + me
            remote(
                outgoing.at[b, to], x_in.at[mine], x_send, x_recv.at[1], 1 - seg, to, 1 - dp
            ).start()
        return carry

    lax.fori_loop(1, count, dispatch_near, 0)
    lax.fori_loop(0, count, dispatch_far, 0)
    for b in range(batches):
        pltpu.make_async_copy(
            outgoing.at[b, me], x_in.at[(dp * 2 + b) * count + me], x_recv.at[0]
        ).start()

    def send_weights(k):
        to_seg, to_dp = z_peers[k]
        remote(
            own_piece, weights.at[k * 2 + core], wz_send.at[k], wz_recv.at[k], to_seg, me, to_dp
        ).start()

    def relay_weights(k):
        block = weights.at[k * 2 + core]
        wait_bytes(block, wz_recv.at[k])
        remote(block, block, wp_send.at[k], wp_recv.at[k], seg, twin, dp).start()

    tail_row[...] = jnp.zeros_like(tail_row)
    for t in range(towers):
        tail_row[0:1, t * per_tower : (t + 1) * per_tower] = tower_out[t : t + 1, :].astype(F32)
    blank = jnp.zeros((own_piece.shape[1] - towers * per_tower, width), BF16)
    stacked = jnp.concatenate([tower_in[t] for t in range(towers)] + [blank], axis=0)
    own_piece[:width, :] = stacked.T
    own_piece[width:, :] = tail_row[...].astype(BF16)
    weights[core] = own_piece[...]
    aux[...] = jnp.zeros_like(aux)
    own_targets = jnp.where(seg == 0, targets[0:1, :], targets[1:2, :])
    own_arms = jnp.where(seg == 0, arms[0:1, :], arms[1:2, :]).astype(F32)
    for odd in range(2):

        @pl.when(lax.rem(chip, 2) == odd)
        def _():
            aux[0:1, odd * rows_here : (odd + 1) * rows_here] = own_targets
            aux[1:2, odd * rows_here : (odd + 1) * rows_here] = own_arms

    remote(own_piece, weights.at[core], wp_send.at[0], wp_recv.at[0], seg, twin, dp).start()
    send_weights(1)

    def send_aux(i, carry):
        to = lax.rem(chip + i, chips)
        remote(aux, aux_in.at[chip], aux_send, aux_recv, seg, to * 2 + core, dp).start()
        return carry

    lax.fori_loop(1, chips, send_aux, 0)
    aux_in[chip] = aux[...]

    def forward(j, carry):
        to_dp = lax.rem(dp + j // 2, 2)
        to_seg = lax.rem(j, 2)
        base = (to_dp * 2 + to_seg) * count

        @pl.when(j == 0)
        def _():
            wait_bytes(x_in.at[pl.ds(dp * 2 * count, 2 * count)], x_recv.at[0])

        @pl.when(j == 2)
        def _():
            wait_bytes(x_in.at[pl.ds((1 - dp) * 2 * count, 2 * count)], x_recv.at[1])

        here = pl.ds(pl.multiple_of(base * capacity, slots), slots)
        rows = wide(x_in[pl.ds(base, count)])
        gate_pre = mm(rows, w_gate[...])
        up_pre = mm(rows, w_up[...])
        sig = sigmoid(gate_pre)
        gated = gate_pre * sig
        act = (gated * up_pre).astype(BF16)
        by_up[here] = gated.astype(BF16)
        by_gate[here] = (up_pre * (sig + gated - gated * sig)).astype(BF16)
        half_hidden = hidden_here // 2
        hidden[0, here] = act[:, :half_hidden]
        hidden[1, here] = act[:, half_hidden:]
        made = mm(act, w_down[...])
        p_out[pl.ds(base, count)] = made.reshape(count, capacity, width).astype(BF16)
        local = (to_dp == dp) & (to_seg == seg)

        def give(i, inner):
            e = lax.rem(me + i, count)

            @pl.when((i > 0) | jnp.logical_not(local))
            def _():
                remote(
                    p_out.at[base + e],
                    r_in.at[z_mine * count + me],
                    p_send,
                    p_recv,
                    to_seg,
                    e,
                    to_dp,
                ).start()

            return inner

        lax.fori_loop(0, count, give, 0)

        @pl.when(local)
        def _():
            pltpu.make_async_copy(
                p_out.at[base + me], r_in.at[z_mine * count + me], p_recv
            ).start()

        return carry

    lax.fori_loop(0, 4, forward, 0)
    top = 272
    halves = ((0, pl.ds(0, top)), (3, pl.ds(top, width + 16 - top)))
    for sem, part in halves:
        remote(
            own_piece.at[part],
            weights.at[6 + core, part],
            wz_send.at[sem],
            wz_recv.at[sem],
            1 - seg,
            me,
            1 - dp,
        ).start()

    def relay_half(sem, part):
        block = weights.at[6 + core, part]
        wait_bytes(block, wz_recv.at[sem])
        remote(
            block, weights.at[4 + core, part], wz_send.at[2], wz_recv.at[2], 1 - seg, me, dp
        ).start()

    relay_weights(1)

    def turn(j, carry):
        here = pl.ds(pl.multiple_of(j * slots, slots), slots)
        x_turned[:, here] = wide(x_in[pl.ds(j * count, count)]).T
        active_turned[: hidden_here // 2, here] = hidden[0, here].T
        active_turned[hidden_here // 2 :, here] = hidden[1, here].T
        return carry

    lax.fori_loop(0, 4, turn, 0)

    wait_bytes(r_in, p_recv)
    own_table = tables[seg]
    added = mm(own_table, wide(r_in[pl.ds(0, count)]))
    for z in range(1, 4):
        added = added + mm(own_table, wide(r_in[pl.ds(z * count, count)]))
    mixed[chip] = (feats[seg].astype(F32) + added).astype(BF16)

    across, along = chip // side, lax.rem(chip, side)
    for ahead in (0, 1, 3, 2):

        def send_rows(i, carry, ahead=ahead):
            to = lax.rem(across + ahead, side) * side + lax.rem(along + i, side)
            block = mixed.at[chip]
            remote(block, block, m_send, m_recv.at[across], seg, to * 2 + core, dp).start()
            return carry

        lax.fori_loop(0 if ahead else 1, side, send_rows, 0)

    depth = width
    out_cols = own_piece.shape[1]
    mask_tower = lax.broadcasted_iota(jnp.int32, (16, out_cols), 0)
    mask_col = lax.broadcasted_iota(jnp.int32, (16, out_cols), 1) // per_tower
    tower_mask = mask_tower == mask_col

    def out_matrix(piece):
        tail = weights[piece, depth:, :].astype(F32)
        return jnp.where(tower_mask, tail[0:1, :], 0.0).astype(BF16)

    def tower_forward(piece, group, fresh):
        here = pl.ds(pl.multiple_of(group * quarter, quarter), quarter)
        blocks = mixed[pl.ds(group * side, side)]
        rows = blocks.reshape(quarter, width)
        pre_act = mm(rows, weights[piece, :depth, :])
        sig = sigmoid(pre_act)
        hid_wide = pre_act * sig
        hid = hid_wide.astype(BF16)
        hidden[piece, here] = hid
        tail = weights[piece, depth:, :].astype(F32)[0:1, :]
        slope[piece, here] = ((sig + hid_wide - hid_wide * sig) * tail).astype(BF16)
        part = mm(out_matrix(piece), hid, NT)
        if fresh:
            values[:, here] = part
        else:
            values[:, here] += part

    wait_bytes(weights.at[0], wp_recv.at[0])
    for j, ahead in enumerate((0, 3, 1, 2)):
        group = lax.rem(across + ahead, side)
        if ahead == 0:
            wait_bytes(mixed.at[pl.ds(0, side - 1)], m_recv.at[group])
        else:
            wait_bytes(mixed.at[pl.ds(0, side)], m_recv.at[group])
        if j == 0:
            wait_bytes(weights.at[0], wp_recv.at[1])
        tower_forward(0, group, True)

        def more(p, carry, group=group):
            tower_forward(p, group, False)
            return carry

        lax.fori_loop(1, 4, more, 0)
        if j == 0:
            relay_half(*halves[0])
        if j == 1:
            relay_half(*halves[1])
            far = weights.at[6 + core]
            remote(far, far, wp_send.at[3], wp_recv.at[3], seg, twin, dp).start()
    for k in (3, 2):
        if k == 2:
            relay_weights(2)
        for turn_core in (core, 1 - core):
            if turn_core is not core:
                wait_bytes(weights.at[0], wp_recv.at[k])

            def more_groups(group, carry, piece=k * 2 + turn_core):
                tower_forward(piece, group, False)
                return carry

            lax.fori_loop(0, side, more_groups, 0)

    wait_bytes(aux_in.at[pl.ds(0, chips - 1)], aux_recv)
    pairs = [aux_in[2 * g] + aux_in[2 * g + 1] for g in range(chips // 2)]
    notes = jnp.concatenate(pairs, axis=1)
    all_targets, all_arms = notes[0:1], notes[1:2]
    all_rows = chips * rows_here
    tower_ids = lax.broadcasted_iota(jnp.int32, (16, all_rows), 0).astype(F32)
    arm_mask = tower_ids - 1.0 == all_arms
    every = values[...]
    value_out[0:1] = every[0:1]
    value_out[1:2] = jnp.sum(jnp.where(arm_mask, every, 0.0), axis=0, keepdims=True)

    def send_values(i, carry):
        to = lax.rem(chip + i, chips)
        remote(value_out, value_in.at[chip], v_send, v_recv, seg, to * 2 + core, dp).start()
        return carry

    lax.fori_loop(1, chips, send_values, 0)
    value_in[chip] = value_out[...]
    for g in range(side):
        mixed_turned[:, g * quarter : (g + 1) * quarter] = (
            mixed[g * side : (g + 1) * side].reshape(quarter, width).T
        )
    wait_bytes(value_in.at[pl.ds(0, chips - 1)], v_recv)
    summed = value_in[0]
    for i in range(1, chips):
        summed = summed + value_in[i]
    treated = jnp.where(all_arms != 0.0, 1.0, 0.0)
    grad_first = loss_scale * (sigmoid(summed[0:1]) - treated)
    grad_arm = loss_scale * (summed[1:2] - all_targets)
    grad_value = jnp.where(tower_ids == 0.0, grad_first, jnp.where(arm_mask, grad_arm, 0.0))
    grad_turned[...] = grad_value.astype(BF16)
    grad_column[...] = grad_value.T.astype(BF16)
    mask_row = jnp.where(tower_mask, 1.0, 0.0).astype(BF16)
    for g in range(side):
        here = slice(g * quarter, (g + 1) * quarter)
        grad_wide[here] = mm(grad_column[here], mask_row).astype(BF16)

    def tower_weight_grad(piece):
        main = mm(mixed_turned[...], slope[piece])
        tail = mm(grad_turned[...], hidden[piece])
        tail = jnp.sum(jnp.where(tower_mask, tail, 0.0), axis=0, keepdims=True)
        tail = jnp.where(mask_tower == 0, tail, 0.0)
        return main, tail

    def twin_grads(k):
        main, tail = tower_weight_grad(k * 2 + 1 - core)
        w_pair_out[k, :depth, :] = main.astype(BF16)
        w_pair_out[k, depth:, :] = tail.astype(BF16)
        remote(
            w_pair_out.at[k], w_pair_in.at[k], tp_send, tp_recv.at[k], seg, twin, dp
        ).start()

    def own_grads(k):
        main, tail = tower_weight_grad(k * 2 + core)
        wait_bytes(w_pair_in.at[k], tp_recv.at[k])
        main = main + w_pair_in[k, :depth, :].astype(F32)
        tail = tail + w_pair_in[k, depth:, :].astype(F32)
        w_z_out[k, :depth, :] = main.astype(BF16)
        w_z_out[k, depth:, :] = tail.astype(BF16)

    inner, outer = (1 - seg, me, dp), (1 - seg, me, 1 - dp)
    upper, lower_part = halves[0][1], halves[1][1]

    def send_piece(k, part, to, sem):
        remote(
            w_z_out.at[k, part], w_z_in.at[k, part], tz_send.at[sem], tz_recv.at[sem], *to
        ).start()

    def add_passing(k, part, sem):
        passing = w_z_in.at[2, part]
        wait_bytes(passing, tz_recv.at[sem])
        w_z_out[k, part] = (w_z_out[k, part].astype(F32) + passing[...].astype(F32)).astype(BF16)

    def slope_to_grad(p, here):
        grad_pre = grad_wide[here] * slope[p, here]
        slope[p, here] = grad_pre
        return grad_pre

    for g in range(side):
        for p in (4, 5):
            slope_to_grad(p, slice(g * quarter, (g + 1) * quarter))

    for j in range(side):
        group = lax.rem(chip // side + (2, 1, 3, 0)[j], side)
        here = pl.ds(pl.multiple_of(group * quarter, quarter), quarter)

        def two(i, total, here=here):
            p = jnp.where(i == 2, 6, 2 * i)
            for q in range(2):
                grad_pre = slope_to_grad(p + q, here)
                total = total + mm(grad_pre, weights[p + q, :depth, :], NT)
            return total

        total = jnp.zeros((quarter, width), F32)
        for p in (4, 5):
            total = total + mm(slope[p, here], weights[p, :depth, :], NT)
        total = lax.fori_loop(0, 3, two, total)
        d_out[pl.ds(group * side, side)] = total.astype(BF16).reshape(side, rows_here, width)

        def send_grads(i, inner, group=group):
            to = group * side + i

            @pl.when(to != chip)
            def _():
                remote(
                    d_out.at[to], d_in.at[chip], d_send, d_recv, seg, to * 2 + core, dp
                ).start()

            return inner

        lax.fori_loop(0, side, send_grads, 0)
        if j == 0:
            twin_grads(2)
        if j == 1:
            own_grads(2)
            send_piece(2, upper, inner, 0)
            send_piece(2, lower_part, outer, 1)
    d_in[chip] = d_out[chip]
    twin_grads(1)
    twin_grads(3)
    own_grads(1)
    send_piece(1, upper, inner, 2)
    own_grads(3)
    send_piece(3, lower_part, outer, 5)

    wait_bytes(d_in.at[pl.ds(0, chips - 1)], d_recv)
    total = d_in[0].astype(F32)
    for i in range(1, chips):
        total = total + d_in[i].astype(F32)
    b_out[...] = mm(own_table, total.astype(BF16), TN).reshape(count, capacity, width).astype(BF16)

    def spread(i, carry):
        e, z = lax.rem(me + i // 4, count), lax.rem(i, 4)
        to_seg, to_dp = lax.rem(seg + lax.rem(z, 2), 2), lax.rem(dp + z // 2, 2)
        remote(
            b_out.at[e], g_in.at[z_mine * count + me], g_send, g_recv.at[z_mine], to_seg, e, to_dp
        ).start()
        return carry

    lax.fori_loop(1, 4 * count, spread, 0)
    pltpu.make_async_copy(b_out.at[me], g_in.at[z_mine * count + me], g_recv.at[z_mine]).start()

    add_passing(3, upper, 0)
    send_piece(3, upper, outer, 4)
    add_passing(1, lower_part, 1)
    send_piece(1, lower_part, inner, 3)
    twin_grads(0)
    own_grads(0)

    def backward(j, carry):
        z = lax.rem(z_mine + j, 4)
        wait_bytes(g_in.at[pl.ds(z * count, count)], g_recv.at[z])
        here = pl.ds(pl.multiple_of(z * slots, slots), slots)
        grads = wide(g_in[pl.ds(z * count, count)])
        g_rows[here] = grads
        grad_active = mm(grads, w_down[...], NT)
        by_gate[here] = (grad_active * by_gate[here].astype(F32)).astype(BF16)
        by_up[here] = (grad_active * by_up[here].astype(F32)).astype(BF16)
        return carry

    lax.fori_loop(0, 4, backward, 0)
    strip = 256

    def gate_grads(j, total):
        cols = pl.ds(pl.multiple_of(j * strip, strip), strip)
        for source, weight, out in ((by_gate, w_gate, out_gate), (by_up, w_up, out_up)):
            grad = mm(x_turned[...], source[:, cols])
            out[:, cols] = grad.astype(BF16)
            term = grad * weight[:, cols].astype(F32)
            for c in range(strip // 128):
                total = total + term[:, c * 128 : (c + 1) * 128]
        return total

    gain_sum = lax.fori_loop(0, hidden_here // strip, gate_grads, jnp.zeros((width, 128), F32))
    gain_row = jnp.sum(gain_sum.T, axis=0, keepdims=True)
    gain_a_out[...] = gain_row / gain[...]
    mine_a = z_mine * 2 + core
    others = []
    for flip_seg in range(2):
        for flip_dp in range(2):
            for flip_core in range(2):
                if flip_seg or flip_dp or flip_core:
                    others.append((flip_seg, flip_dp, flip_core))
    for flip_seg, flip_dp, flip_core in others:
        remote(
            gain_a_out,
            gain_a_in.at[mine_a],
            ga_send,
            ga_recv,
            1 - seg if flip_seg else seg,
            twin if flip_core else me,
            1 - dp if flip_dp else dp,
        ).start()
    gain_a_in[mine_a] = gain_a_out[...]

    def down_grads(j, carry):
        here = pl.ds(pl.multiple_of(j * strip, strip), strip)
        out_down[here] = mm(active_turned[here], g_rows[...]).astype(BF16)
        return carry

    half = hidden_here // strip // 2
    lax.fori_loop(0, half, down_grads, 0)
    wait_bytes(gain_a_in.at[pl.ds(0, 7)], ga_recv)
    part = gain_a_in[0]
    for i in range(1, 8):
        part = part + gain_a_in[i]
    gain_b_out[...] = part

    def send_gain(i, carry):
        to = lax.rem(chip + i, chips)
        remote(gain_b_out, gain_b_in.at[chip], gb_send, gb_recv, seg, to * 2 + core, dp).start()
        return carry

    lax.fori_loop(1, chips, send_gain, 0)
    gain_b_in[chip] = gain_b_out[...]
    lax.fori_loop(half, hidden_here // strip, down_grads, 0)

    tower_sum = w_z_out[0].astype(F32)
    for k, part, sem in (
        (1, upper, 2),
        (1, lower_part, 3),
        (3, upper, 4),
        (3, lower_part, 5),
    ):
        wait_bytes(w_z_in.at[k, part], tz_recv.at[sem])
    for k in (1, 3):
        tower_sum = tower_sum + w_z_in[k].astype(F32)
    turned_sum = tower_sum[:width].T
    for t in range(towers):
        here = slice(t * per_tower, (t + 1) * per_tower)
        out_tower[t] = turned_sum[here].astype(BF16)
        sum_row[t : t + 1, :] = tower_sum[width : width + 1, here]
    out_tower_row[...] = sum_row[0:towers, :].astype(BF16)
    wait_bytes(gain_b_in.at[pl.ds(0, chips - 1)], gb_recv)
    part = gain_b_in[0]
    for i in range(1, chips):
        part = part + gain_b_in[i]
    out_gain[...] = part

    wait_bytes(x_in.at[pl.ds(0, 4 * count - 2)], x_send)
    wait_bytes(aux_in.at[pl.ds(0, chips - 1)], aux_send)
    wait_bytes(r_in.at[pl.ds(0, 4 * count - 1)], p_send)
    wait_bytes(mixed.at[pl.ds(0, chips - 1)], m_send)
    wait_bytes(value_in.at[pl.ds(0, chips - 1)], v_send)
    wait_bytes(d_in.at[pl.ds(0, chips - 1)], d_send)
    wait_bytes(g_in.at[pl.ds(0, 4 * count - 1)], g_send)
    for sem, part in enumerate((upper, lower_part, upper, lower_part, upper, lower_part)):
        wait_bytes(own_piece.at[part], tz_send.at[sem])
    for sem, part in halves:
        wait_bytes(own_piece.at[part], wz_send.at[sem])
    wait_bytes(own_piece, wz_send.at[1])
    wait_bytes(own_piece, wz_send.at[2])
    for k in range(4):
        wait_bytes(own_piece, wp_send.at[k])
    wait_bytes(w_pair_in, tp_send)
    wait_bytes(gain_a_in.at[pl.ds(0, 7)], ga_send)
    wait_bytes(gain_b_in.at[pl.ds(0, chips - 1)], gb_send)


def run_step(loss_scale, count, capacity, *args):
    feats, routes, arms, targets, gain, w_gate, w_up, w_down, tower_in, tower_out = args
    batches, rows_here, width = feats.shape
    hidden_here = w_gate.shape[2]
    cols = 8 * tower_in.shape[1]
    piece = jax.ShapeDtypeStruct((width + 16, cols), BF16)
    chips = count // 2
    blocks = 4 * count
    slots = blocks * capacity
    all_rows = chips * rows_here
    v = pltpu.VMEM
    dma = pltpu.SemaphoreType.DMA
    scratch = [
        v((8, 2 * rows_here), F32),
        v(piece.shape, BF16),
        v((16, cols), F32),
        v((8, tower_in.shape[1]), F32),
        v((all_rows, cols), BF16),
        v((batches, rows_here, count * capacity), BF16),
        v((batches, count, capacity, width), BF16),
        v((blocks, capacity, width), BF16),
        v((width, slots), BF16),
        v((slots, hidden_here), BF16),
        v((slots, hidden_here), BF16),
        v((hidden_here, slots), BF16),
        v((blocks, capacity, width), BF16),
        v((blocks, capacity, width), BF16),
        v((chips, rows_here, width), BF16),
        v((width, all_rows), BF16),
        v((chips, 8, 128), F32),
        v((8,) + piece.shape, BF16),
        v((8, all_rows, cols), BF16),
        v((8, all_rows, cols), BF16),
        v((16, all_rows), F32),
        v((2, all_rows), F32),
        v((chips, 2, all_rows), F32),
        v((16, all_rows), BF16),
        v((all_rows, 16), BF16),
        v((chips, rows_here, width), BF16),
        v((chips, rows_here, width), BF16),
        v((count, capacity, width), BF16),
        v((blocks, capacity, width), BF16),
        v((slots, width), BF16),
        v((4,) + piece.shape, BF16),
        v((4,) + piece.shape, BF16),
        v((4,) + piece.shape, BF16),
        v((4,) + piece.shape, BF16),
        v((1, width), F32),
        v((8, 1, width), F32),
        v((1, width), F32),
        v((chips, 1, width), F32),
        dma(()),
        dma((2,)),
        dma(()),
        dma(()),
        dma(()),
        dma(()),
        dma(()),
        dma((4,)),
        dma(()),
        dma(()),
        dma(()),
        dma(()),
        dma(()),
        dma((4,)),
        dma((4,)),
        dma((4,)),
        dma((4,)),
        dma((4,)),
        dma(()),
        dma((4,)),
        dma((6,)),
        dma((6,)),
        dma(()),
        dma(()),
        dma(()),
        dma(()),
    ]
    out_shape = (
        jax.ShapeDtypeStruct(w_gate.shape, BF16),
        jax.ShapeDtypeStruct(w_up.shape, BF16),
        jax.ShapeDtypeStruct(w_down.shape, BF16),
        jax.ShapeDtypeStruct(tower_in.shape, BF16),
        jax.ShapeDtypeStruct(tower_out.shape, BF16),
        jax.ShapeDtypeStruct((1, width), F32),
    )
    spec = pl.BlockSpec(memory_space=pltpu.VMEM)
    return pl.pallas_call(
        functools.partial(step_kernel, loss_scale),
        out_shape=out_shape,
        in_specs=[spec] * len(args),
        out_specs=(spec,) * len(out_shape),
        scratch_shapes=scratch,
        compiler_params=pltpu.CompilerParams(
            collective_id=0, has_side_effects=True, vmem_limit_bytes=67043328
        ),
    )(*args)


def body(
    features,
    routes,
    arm_ids,
    targets,
    trunk_gain,
    gate_weight,
    up_weight,
    down_weight,
    tower_in,
    tower_out,
):
    batches, rows_here, width = features.shape
    count = lax.axis_size("expert")
    capacity = max(2, 2 * routes.shape[2] * rows_here // count)
    loss_scale = float(batches * rows_here * count * lax.axis_size("dp")) ** (-0.5)
    *grads, grad_gain = run_step(
        loss_scale,
        count,
        capacity,
        features,
        routes.transpose(0, 2, 1),
        arm_ids,
        targets,
        trunk_gain.reshape(1, width),
        gate_weight,
        up_weight,
        down_weight,
        tower_in.transpose(0, 2, 1),
        tower_out,
    )
    grads[3] = grads[3].transpose(0, 2, 1)
    return (*grads, grad_gain.reshape(width))


def solution(mesh):
    in_specs = (
        P(None, ("expert", "dp"), None),
        P(None, ("expert", "dp"), None),
        P(None, ("expert", "dp")),
        P(None, ("expert", "dp")),
        P(),
        P("expert", None, ("segment", "dp")),
        P("expert", None, ("segment", "dp")),
        P("expert", ("segment", "dp"), None),
        P(None, None, ("segment", "expert", "dp")),
        P(None, ("segment", "expert", "dp")),
    )
    out_specs = (
        P("expert", None, ("segment", "dp")),
        P("expert", None, ("segment", "dp")),
        P("expert", ("segment", "dp"), None),
        P(None, None, ("segment", "expert", "dp")),
        P(None, ("segment", "expert", "dp")),
        P(),
    )
    return jax.shard_map(body, mesh=mesh, in_specs=in_specs, out_specs=out_specs, check_vma=False)
```
